512 devices in a mesh: gx: 16 (over x, z_hi, core), gy: 4 (over y), gz: 8 (over z_lo).
Axes of the slice: x: 4, y: 4, z: 16 (z_hi: 2, z_lo: 8; z = z_hi * 8 + z_lo), core: 2. Of those that a mesh axis runs over, the one named last changes fastest.
Arguments:
- positions: float32 [3, 32768], P(None, ('gx', 'gy', 'gz')), may hold values from 0 to 6
- species: int32 [32768], P(('gx', 'gy', 'gz')), may hold values from 0 to 6
- counts: int32 [512], P(('gx', 'gy', 'gz')), may hold values from 16 to 64, as said below
- neighbours: int32 [32, 32768], P(None, ('gx', 'gy', 'gz')), may hold values from 0 to 495, as said below
- exports: int32 [8192], P(('gx', 'gy', 'gz')), may hold values from 0 to 63, as said below
- embedding: bfloat16 [7, 128], replicated, may hold values from -5 to 5
- radial_in: bfloat16 [2, 8, 64], replicated, may hold values from -2 to 2
- radial_out_one: bfloat16 [64, 256], replicated, may hold values from -0.75 to 0.75
- radial_out_two: bfloat16 [64, 512], replicated, may hold values from -0.75 to 0.75
- mix_one: bfloat16 [6, 128, 128], replicated, may hold values from -0.5 to 0.5
- mix_two: bfloat16 [5, 128, 128], replicated, may hold values from -0.5 to 0.5
- readout: float32 [2, 128], replicated, may hold values from -0.5 to 0.5
Outputs:
- forces: float32 [3, 32768], P(None, ('gx', 'gy', 'gz'))
- site_energies: float32 [32768], P(('gx', 'gy', 'gz'))
The draws below stay inside these ranges and needn't reach their ends.
Inputs may be any that keep to these rules, and one draw needn't show every extreme that they name: `counts`: one domain in each draw holds exactly 64 live atoms; the others are spread with many near 64 // 4. `neighbours`: column i of domain d lists table indices: live local slots other than i, or 64 + b * 16 + e with b never 13. Entries equal to i are padding; columns of slots at or past the domain's count hold only i. Slot 0 of every domain has 32 entries other than itself. `exports`: the 16 entries of a domain are distinct slots below its count.
All inputs are finite; a program needn't handle non-finite values.
Results may differ from the reference program's by a relative error of at most 0.025.
Values may be sent and summed in bfloat16 or wider, within the bound.
No kernel may reach another device: no remote copies, remote signals or barrier semaphores. Data moves between devices by JAX's collectives and lax.ppermute only.
A program may use at most 64 MiB of HBM per device.

```python
import math
import jax
import jax.numpy as jnp
import numpy as np
from jax import lax

C = 128
NB = 8
RH = 64
NSPEC = 7
SLOTS = 64
MAXNB = 32
EXPORT = 16
ATOMS = 32768
N_GX = 16
N_GY = 4
N_GZ = 8


def domain_counts(key):
    domains = N_GX * N_GY * N_GZ
    picks = jax.random.randint(jax.random.fold_in(key, 11), (domains,), 0, 65)
    spread = (SLOTS - SLOTS // 4) * picks * picks * picks // (64 * 64 * 64)
    fullest = jax.random.randint(jax.random.fold_in(key, 12), (), 0, domains)
    return jnp.where(jnp.arange(domains) == fullest, SLOTS, SLOTS // 4 + spread).astype(jnp.int32)


def draw_counts(key, part):
    return domain_counts(key)


def draw_neighbours(key, part):
    domains = N_GX * N_GY * N_GZ
    counts = domain_counts(key)
    shape = (MAXNB, domains, SLOTS)
    slot_ids = jnp.broadcast_to(jnp.arange(SLOTS, dtype=jnp.int32)[None, None, :], shape)
    lengths = jax.random.randint(jax.random.fold_in(key, 21), (domains, SLOTS), MAXNB // 2, MAXNB + 1)
    lengths = lengths.at[:, 0].set(MAXNB)
    kinds = jax.random.randint(jax.random.fold_in(key, 22), shape, 0, 3)
    local_pick = jax.random.randint(jax.random.fold_in(key, 23), shape, 0, jnp.broadcast_to(counts[None, :, None] - 1, shape))
    local_pick = local_pick + (local_pick >= slot_ids).astype(jnp.int32)
    block_pick = jax.random.randint(jax.random.fold_in(key, 24), shape, 0, 26)
    block_pick = block_pick + (block_pick >= 13).astype(jnp.int32)
    entry_pick = jax.random.randint(jax.random.fold_in(key, 25), shape, 0, EXPORT)
    ghost = SLOTS + block_pick * EXPORT + entry_pick
    chosen = jnp.where(kinds == 0, local_pick, ghost)
    ranks = jnp.arange(MAXNB, dtype=jnp.int32)[:, None, None]
    used = (ranks < lengths[None]) & (slot_ids < counts[None, :, None])
    result = jnp.where(used, chosen, slot_ids)
    result = result.at[MAXNB - 1, :, 0].set(SLOTS + 27 * EXPORT - 1)
    result = result.at[0, :, 1].set(0)
    return result.reshape(MAXNB, domains * SLOTS).astype(jnp.int32)


def draw_exports(key, part):
    domains = N_GX * N_GY * N_GZ
    counts = domain_counts(key)
    scores = jax.random.randint(jax.random.fold_in(key, 31), (domains, SLOTS), 0, 1048576)
    slot_ids = jnp.arange(SLOTS, dtype=jnp.int32)[None, :]
    keyed = jnp.where(slot_ids < counts[:, None], scores * SLOTS + slot_ids, 1073741824 + slot_ids)
    keyed = jnp.where(slot_ids == 0, -2, keyed)
    keyed = jnp.where((slot_ids == SLOTS - 1) & (counts[:, None] == SLOTS), -1, keyed)
    ordered = jnp.argsort(keyed, axis=1, stable=True)[:, :EXPORT]
    return ordered.reshape(domains * EXPORT).astype(jnp.int32)


def place_ends(array, own_key, low, high):
    index_at = [jax.random.randint(jax.random.fold_in(own_key, axis), (), 0, length) for axis, length in enumerate(array.shape)]
    widest = array.shape.index(max(array.shape))
    beside = index_at[:widest] + [(index_at[widest] + 1) % array.shape[widest]] + index_at[widest + 1:]
    return array.at[tuple(index_at)].set(low).at[tuple(beside)].set(high)


def levels(own_key, shape, shards, low, top_value):
    level = 1.0
    for axis_at, parts in shards:
        steps = jax.random.uniform(jax.random.fold_in(jax.random.fold_in(own_key, 6), axis_at), (parts,), jnp.float32, low / len(shards), top_value / len(shards))
        level = level * jnp.repeat(jnp.exp(steps), shape[axis_at] // parts).reshape((-1,) + (1,) * (len(shape) - 1 - axis_at))
    return level


def cumulative_ranks(number_of, skew):
    portions = [(1 << 20) // math.isqrt(grade ** skew) + 1 for grade in range(1, number_of + 1)]
    scale = 1 + sum(portions) // (1 << 30)
    return np.cumsum(np.array([max(1, weight // scale) for weight in portions]))


def skewed_ids(rng, dims, number_of, skew):
    table = cumulative_ranks(number_of, skew)
    ticket = jax.random.randint(jax.random.fold_in(rng, 1), dims, 0, int(table[number_of - 1]))
    standing = jnp.searchsorted(jnp.asarray(table, jnp.int32), ticket, side="right")
    return jax.random.permutation(jax.random.fold_in(rng, 2), number_of)[standing].astype(jnp.int32)


def bell_draw(key, shape, scale, most, kind=jnp.bfloat16):
    values = jax.random.normal(key, shape, jnp.float32) * scale
    return jnp.minimum(jnp.maximum(values, -most), most).astype(kind)


def setup_inputs(seed: int = 0) -> dict:
    streams_of = jax.random.split(jax.random.key(seed), 13)
    positions = jnp.clip(6.0 * jax.random.uniform(streams_of[0], (3, ATOMS), jnp.float32) ** levels(streams_of[0], (3, ATOMS), ((1, 512),), -0.2, 0.2), 0.0, 6.0)
    species = place_ends(skewed_ids(streams_of[1], (ATOMS,), NSPEC, 2), jax.random.fold_in(streams_of[1], 3), 0, NSPEC - 1).astype(jnp.int32)
    counts = draw_counts(jax.random.fold_in(streams_of[12], 71), 0)
    neighbours = draw_neighbours(jax.random.fold_in(streams_of[12], 71), 0)
    exports = draw_exports(jax.random.fold_in(streams_of[12], 71), 0)
    embedding = bell_draw(streams_of[5], (NSPEC, C), 1.0, 5.0)
    radial_in = bell_draw(streams_of[6], (2, NB, RH), NB ** -0.5, 2.0)
    radial_out_one = bell_draw(streams_of[7], (RH, 2 * C), RH ** -0.5, 0.75)
    radial_out_two = bell_draw(streams_of[8], (RH, 4 * C), RH ** -0.5, 0.75)
    mix_one = bell_draw(streams_of[9], (6, C, C), C ** -0.5, 0.5)
    mix_two = bell_draw(streams_of[10], (5, C, C), C ** -0.5, 0.5)
    readout = bell_draw(streams_of[11], (2, C), C ** -0.5, 0.5, jnp.float32)
    return dict(positions=positions, species=species, counts=counts, neighbours=neighbours, exports=exports, embedding=embedding, radial_in=radial_in, radial_out_one=radial_out_one, radial_out_two=radial_out_two, mix_one=mix_one, mix_two=mix_two, readout=readout)


DOMAIN_LENGTH = 6.0
CUTOFF = 6.0
SOFTEN = 0.25

def mixed(values, matrix):
    return jnp.dot(values, matrix.astype(jnp.float32), precision=lax.Precision.HIGHEST)

def pair_terms(positions_all, neighbour_rows, first_row, live_count, radial_first, radial_second):
    list_depth, block_rows = neighbour_rows.shape
    receivers = first_row + jnp.arange(block_rows, dtype=jnp.int32)
    centre = lax.dynamic_slice_in_dim(positions_all, first_row, block_rows, 1)
    others = jnp.take(positions_all, neighbour_rows, axis=1)
    offset_vec = others - centre[:, None, :]
    distance = jnp.sqrt(lax.optimization_barrier(jnp.sum(offset_vec * offset_vec, axis=0)) + SOFTEN)
    live_rows = (receivers < live_count).astype(jnp.float32)
    paired = (neighbour_rows != receivers[None, :]).astype(jnp.float32) * live_rows[None, :]
    direction = jnp.moveaxis(offset_vec / distance[None], 0, -1)[..., None]
    orders = jnp.arange(1, NB + 1).astype(jnp.float32)[:, None, None]
    scaled = jnp.minimum(distance / CUTOFF, 1.0)
    envelope = 1.0 - 28.0 * scaled ** 6 + 48.0 * scaled ** 7 - 21.0 * scaled ** 8
    basis_rows = jnp.sin(orders * (math.pi / CUTOFF) * distance[None]) / distance[None] * (envelope * paired)[None]
    flattened = basis_rows.reshape(NB, list_depth * block_rows).T.astype(jnp.bfloat16)
    hidden = jax.nn.silu(jnp.dot(flattened, radial_first, preferred_element_type=jnp.float32)).astype(jnp.bfloat16)
    radial = jnp.dot(hidden, radial_second, preferred_element_type=jnp.float32)
    radial = radial.reshape(list_depth, block_rows, radial_second.shape[1] // C, C)
    return (radial, direction, 1.0 / math.sqrt(list_depth), live_rows)

def layer_one(positions_all, projected, own_scalar, neighbour_rows, first_row, live_count, radial_first, radial_second, mixing, readout_row):
    radial, direction, norm_factor, live_rows = pair_terms(positions_all, neighbour_rows, first_row, live_count, radial_first, radial_second)
    source = jnp.take(projected, neighbour_rows, axis=0)
    first_sum = lax.optimization_barrier(jnp.sum(radial[:, :, 0] * source, axis=0)) * norm_factor
    second_sum = lax.optimization_barrier(jnp.sum(radial[:, :, 1, None] * source[:, :, None] * direction, axis=0)) * norm_factor
    quadratic = lax.optimization_barrier(jnp.sum(second_sum * second_sum, axis=1))
    scalar_out = own_scalar + mixed(first_sum, mixing[1]) + mixed(first_sum * first_sum, mixing[2]) + mixed(quadratic, mixing[3])
    vector_out = mixed(second_sum, mixing[4]) + mixed(first_sum[:, None] * second_sum, mixing[5])
    energy = jnp.dot(scalar_out, readout_row, precision=lax.Precision.HIGHEST) * live_rows
    return (jnp.concatenate([scalar_out[:, None], vector_out], axis=1), energy)

def layer_two(positions_all, projected, own_scalar, neighbour_rows, first_row, live_count, radial_first, radial_second, mixing, readout_row):
    radial, direction, norm_factor, live_rows = pair_terms(positions_all, neighbour_rows, first_row, live_count, radial_first, radial_second)
    source = jnp.take(projected, neighbour_rows, axis=0)
    scalar_src = source[:, :, 0]
    vector_src = source[:, :, 1:]
    along_unit = lax.optimization_barrier(jnp.sum(vector_src * direction, axis=2))
    first_sum = lax.optimization_barrier(jnp.sum(radial[:, :, 0] * scalar_src + radial[:, :, 3] * along_unit, axis=0)) * norm_factor
    second_sum = lax.optimization_barrier(jnp.sum(radial[:, :, 1, None] * scalar_src[:, :, None] * direction + radial[:, :, 2, None] * vector_src, axis=0)) * norm_factor
    quadratic = lax.optimization_barrier(jnp.sum(second_sum * second_sum, axis=1))
    scalar_out = own_scalar + mixed(first_sum, mixing[2]) + mixed(first_sum * first_sum, mixing[3]) + mixed(quadratic, mixing[4])
    return jnp.dot(scalar_out, readout_row, precision=lax.Precision.HIGHEST) * live_rows

def project_two(features, mixing):
    return jnp.concatenate([mixed(features[:, :1], mixing[0]), mixed(features[:, 1:], mixing[1])], axis=1)

def reference(positions, species, counts, neighbours, exports, embedding, radial_in, radial_out_one, radial_out_two, mix_one, mix_two, readout):
    domains = N_GX * N_GY * N_GZ
    domain_ids = jnp.arange(domains, dtype=jnp.int32)
    place_x = domain_ids // (N_GY * N_GZ)
    place_y = domain_ids // N_GZ % N_GY
    place_z = domain_ids % N_GZ
    block_ids = jnp.arange(27, dtype=jnp.int32)
    step_x = block_ids // 9 - 1
    step_y = block_ids // 3 % 3 - 1
    step_z = block_ids % 3 - 1
    owners = ((place_x[:, None] + step_x[None]) % N_GX * N_GY + (place_y[:, None] + step_y[None]) % N_GY) * N_GZ + (place_z[:, None] + step_z[None]) % N_GZ
    export_table = exports.reshape(domains, EXPORT)
    ghost_index = owners[:, :, None] * SLOTS + export_table[owners]
    slot_ids = jnp.arange(SLOTS, dtype=jnp.int32)
    own_index = domain_ids[:, None] * SLOTS + slot_ids[None]
    table_index = jnp.concatenate([own_index, ghost_index.reshape(domains, 27 * EXPORT)], axis=1).astype(jnp.int32)
    move_vectors = jnp.stack([step_x, step_y, step_z]).astype(jnp.float32) * DOMAIN_LENGTH
    ghost_shift = jnp.broadcast_to(move_vectors[:, :, None], (3, 27, EXPORT)).reshape(3, 27 * EXPORT)
    table_shift = jnp.concatenate([jnp.zeros((3, SLOTS), jnp.float32), ghost_shift], axis=1)

    def domain_inputs(domain):
        lookup = table_index[domain]
        where_atoms = jnp.take(positions, lookup, axis=1) + table_shift
        neighbour_rows = lax.dynamic_slice_in_dim(neighbours, domain * SLOTS, SLOTS, 1)
        return (lookup, where_atoms, neighbour_rows, counts[domain])

    def first_inputs(lookup):
        scalar0 = jnp.take(embedding, jnp.take(species, lookup), axis=0).astype(jnp.float32)
        return (scalar0, mixed(scalar0, mix_one[0]))

    def first_layer(domain):
        lookup, where_atoms, neighbour_rows, live_count = domain_inputs(domain)
        scalar0, projected = first_inputs(lookup)
        return layer_one(where_atoms, projected, scalar0[:SLOTS], neighbour_rows, 0, live_count, radial_in[0], radial_out_one, mix_one, readout[0])
    features1, energy1 = lax.map(first_layer, domain_ids)
    rounded = lax.optimization_barrier(features1.astype(jnp.bfloat16)).astype(jnp.float32).reshape(domains * SLOTS, 4, C)

    def second_layer(running, domain):
        grad_pos, grad_feat = running
        lookup, where_atoms, neighbour_rows, live_count = domain_inputs(domain)
        live = (slot_ids < live_count).astype(jnp.float32)
        table_feat = jnp.take(rounded, lookup, axis=0)

        def energy_of(atoms_at, table_rows):
            projected = project_two(table_rows, mix_two)
            return layer_two(atoms_at, projected, table_rows[:SLOTS, 0], neighbour_rows, 0, live_count, radial_in[1], radial_out_two, mix_two, readout[1])
        energy2, pullback = jax.vjp(energy_of, where_atoms, table_feat)
        grad_atoms, grad_rows = pullback(live)
        return ((grad_pos.at[:, lookup].add(grad_atoms), grad_feat.at[lookup].add(grad_rows)), energy2)
    start_state = (jnp.zeros((3, domains * SLOTS), jnp.float32), jnp.zeros((domains * SLOTS, 4, C), jnp.float32))
    (grad_pos, grad_feat), energy2 = lax.scan(second_layer, start_state, domain_ids)

    def first_backward(grad_total, domain):
        lookup, where_atoms, neighbour_rows, live_count = domain_inputs(domain)
        live = (slot_ids < live_count).astype(jnp.float32)
        scalar0, projected = first_inputs(lookup)

        def features_of(atoms_at):
            return layer_one(atoms_at, projected, scalar0[:SLOTS], neighbour_rows, 0, live_count, radial_in[0], radial_out_one, mix_one, readout[0])
        unused, pullback = jax.vjp(features_of, where_atoms)
        cotangent = lax.dynamic_slice_in_dim(grad_feat, domain * SLOTS, SLOTS, 0)
        grad_atoms, = pullback((cotangent, live))
        return (grad_total.at[:, lookup].add(grad_atoms), energy1[0, 0])
    grad_pos, unused = lax.scan(first_backward, grad_pos, domain_ids)
    live_all = (slot_ids[None, :] < counts[:, None]).astype(jnp.float32)
    site_energies = (live_all * (energy1 + energy2)).reshape(domains * SLOTS)
    return (-grad_pos, site_energies)
```

```python
import math

import jax
import jax.numpy as jnp
from jax import lax
from jax.experimental import pallas as pl
from jax.experimental.pallas import tpu as pltpu
from jax.sharding import PartitionSpec as P

C = 128
NB = 8
RH = 64
NSPEC = 7
SLOTS = 64
DEPTH = 32
EXPORT = 16
PAIRS = SLOTS * DEPTH
SLAB = 9 * EXPORT
TABLE = 512
LANES = 128
COLUMNS = PAIRS // LANES
DOMAIN_LENGTH = 6.0
CUTOFF = 6.0
SOFTEN = 0.25
NORM = 1.0 / math.sqrt(DEPTH)
AXES = ("gx", "gy", "gz")
F32 = jnp.float32
BF16 = jnp.bfloat16


def dot_nn(a, b):
    return lax.dot_general(a, b, (((1,), (0,)), ((), ())), preferred_element_type=F32)


def dot_nt(a, b):
    return lax.dot_general(a, b, (((1,), (1,)), ((), ())), preferred_element_type=F32)


def dot_tn(a, b):
    return lax.dot_general(a, b, (((0,), (0,)), ((), ())), preferred_element_type=F32)


def iota(shape, dim):
    return lax.broadcasted_iota(jnp.int32, shape, dim)


def column(values, m):
    return values[:, m * LANES : (m + 1) * LANES]


def halves(values):
    high = values.astype(BF16)
    low = (values - high.astype(F32)).astype(BF16)
    return jnp.where(iota(values.shape, 1) % LANES < SLOTS, high.astype(F32), low.astype(F32)).astype(BF16)


def fold(values):
    return values + pltpu.roll(values, SLOTS, 1)


def live_row(count):
    return (iota((1, LANES), 1) % SLOTS < count).astype(F32)


def gather_entries(table, index):
    parts = []
    for m in range(COLUMNS):
        ids = jnp.broadcast_to(column(index, m), (8, LANES))
        low = ids & (LANES - 1)
        high = ids >> 7
        found = jnp.take_along_axis(column(table, 0), low, axis=1)
        for v in range(1, TABLE // LANES):
            found = jnp.where(high == v, jnp.take_along_axis(column(table, v), low, axis=1), found)
        parts.append(found)
    return jnp.concatenate(parts, axis=1)


def sincos_pi(turns):
    whole = jnp.floor(turns + 0.5)
    part = turns - whole
    sign = 1.0 - 2.0 * (whole - 2.0 * jnp.floor(whole * 0.5))
    square = part * part
    sine = 0.0
    cosine = 0.0
    for n in range(6, -1, -1):
        cosine = cosine * square + (-1.0) ** n * math.pi ** (2 * n) / math.factorial(2 * n)
    for n in range(5, -1, -1):
        sine = sine * square + (-1.0) ** n * math.pi ** (2 * n + 1) / math.factorial(2 * n + 1)
    return sine * part * sign, cosine * sign


def geometry(table, index, count, with_slope):
    found = gather_entries(table, index)
    first = column(table, 0)
    centre = jnp.where(iota((8, LANES), 1) < SLOTS, first, pltpu.roll(first, SLOTS, 1))
    centre = jnp.concatenate([centre] * COLUMNS, axis=1)
    rows = iota((8, PAIRS), 0)
    delta = jnp.where(rows < 3, found - centre, 0.0)
    kind = found[3:4, :]
    square = jnp.sum(delta * delta, axis=0, keepdims=True) + SOFTEN
    inverse = lax.rsqrt(square)
    distance = square * inverse
    unit = delta * inverse
    slot = iota((1, PAIRS), 1) % SLOTS
    paired = jnp.where((index != slot) & (slot < count), 1.0, 0.0)
    scaled = jnp.minimum(distance * (1.0 / CUTOFF), 1.0)
    power = scaled * scaled * scaled
    power = power * power
    envelope = 1.0 + power * (-28.0 + scaled * (48.0 - 21.0 * scaled))
    orders = (iota((8, 1), 0) + 1).astype(F32)
    sine, cosine = sincos_pi(orders * scaled)
    weight = envelope * paired * inverse
    basis = (sine * weight).astype(BF16)
    if not with_slope:
        return unit, inverse, kind, basis, None
    rest = 1.0 - scaled
    slope = (-168.0 / CUTOFF) * (power * rest * rest) / jnp.maximum(scaled, 1e-3)
    basis_slope = weight * cosine * (orders * (math.pi / CUTOFF)) + sine * (
        slope * paired * inverse - weight * inverse
    )
    return unit, inverse, kind, basis, basis_slope


def hidden_of(weights, basis):
    before = dot_nn(weights, basis)
    gate = 1.0 / (1.0 + jnp.exp(-before))
    return before, gate


def pair_gradient(unit, inverse, grad_unit, grad_distance):
    along = jnp.sum(grad_unit * unit, axis=0, keepdims=True)
    return inverse * (grad_unit - unit * along) + unit * grad_distance


def stack_rows(rows):
    where = iota((8, rows[0].shape[1]), 0)
    out = jnp.zeros((8, rows[0].shape[1]), F32)
    for r, row in enumerate(rows):
        out = jnp.where(where == r, row, out)
    return out


def start_kernel(exports, positions, species, own, payload, picked):
    own[...] = jnp.zeros_like(own)
    own[0:3, 0:SLOTS] = positions[...]
    own[3:4, 0:SLOTS] = species[...].astype(F32)
    lane = iota((8, LANES), 1) % EXPORT
    row = iota((EXPORT, LANES), 0)
    source = jnp.zeros((8, LANES), jnp.int32)
    pick = jnp.zeros((EXPORT, LANES), jnp.int32)
    for e in range(EXPORT):
        slot = exports[e]
        source = jnp.where(lane == e, slot, source)
        pick = jnp.where(row == e, slot, pick)
    picked[...] = pick
    payload[...] = jnp.take_along_axis(own[...], source, axis=1)


def first_kernel(
    count_ref, own, low, mid, high, index, picked, win_t, wout_t, mix_a, mix_b, mix0_t, emb, emb_t, read_t,
    table, own_rows, outgoing, sums, energy, spread, radial,
):
    count = count_ref[0]
    group = iota((8, LANES), 1) // EXPORT
    rows8 = iota((8, 1), 0)
    tiles = [own[...]] + [jnp.zeros((8, LANES), F32) for _ in range(3)]
    slabs = (low, mid, high)
    for b in range(27):
        oz, oy, ox = b // 9 - 1, b // 3 % 3 - 1, b % 3 - 1
        entry = SLOTS + b * EXPORT
        shift = jnp.where(rows8 == 0, DOMAIN_LENGTH * ox, 0.0)
        shift = jnp.where(rows8 == 1, DOMAIN_LENGTH * oy, shift)
        shift = jnp.where(rows8 == 2, DOMAIN_LENGTH * oz, shift)
        tile = entry // LANES
        at = entry % LANES // EXPORT
        tiles[tile] = jnp.where(group == at, slabs[oz + 1][b % 9] + shift, tiles[tile])
    for v in range(4):
        table[:, v * LANES : (v + 1) * LANES] = tiles[v]
    whole = jnp.concatenate(tiles, axis=1)
    ids = index[...]
    unit, inverse, kind, basis, _ = geometry(whole, ids, count, False)
    before, gate = hidden_of(win_t[...], basis)
    hidden = (before * gate).astype(BF16)
    pe = dot_nt(mix0_t[...], emb[...])
    pe_high = pe.astype(BF16)
    pe_low = (pe - pe_high.astype(F32)).astype(BF16)
    pe_both = jnp.concatenate([pe_high.astype(F32), pe_low.astype(F32)], axis=1).astype(BF16)
    spread[...] = pe_both
    species = (iota((16, PAIRS), 0) % 8 == kind.astype(jnp.int32)).astype(F32).astype(BF16)
    a0 = jnp.zeros((C, LANES), F32)
    a1 = [jnp.zeros((C, LANES), F32) for _ in range(3)]
    for m in range(COLUMNS):
        radial = dot_nn(wout_t[...], column(hidden, m))
        source = dot_nn(pe_both, column(species, m))
        a0 = a0 + radial[:C] * source
        t = radial[C:] * source
        for x in range(3):
            a1[x] = a1[x] + t * column(unit[x : x + 1], m)
    a0 = fold(a0) * NORM
    a1 = [fold(v) * NORM for v in a1]
    for x, v in enumerate([a0] + a1):
        sums[x * C : (x + 1) * C, :] = v
    quad = a1[0] * a1[0] + a1[1] * a1[1] + a1[2] * a1[2]
    own_kind = (iota((8, LANES), 0) == whole[3:4, :LANES].astype(jnp.int32)).astype(F32).astype(BF16)
    own_kind = jnp.where(iota((8, LANES), 1) < SLOTS, own_kind.astype(F32), 0.0).astype(BF16)
    scalar = dot_nn(emb_t[...], own_kind)
    scalar = scalar + dot_nn(mix_a[...], jnp.concatenate([halves(a0), halves(a0 * a0), halves(quad)], axis=0))
    scalar = fold(scalar)
    top = jnp.concatenate([halves(v) for v in a1], axis=1)
    bottom = jnp.concatenate([halves(a0 * v) for v in a1], axis=1)
    vector = dot_nn(mix_b[...], jnp.concatenate([top, bottom], axis=0))
    parts = [scalar] + [fold(column(vector, x)) for x in range(3)]
    features = jnp.concatenate(parts, axis=0).astype(BF16)
    rounded = features[:C].astype(F32)
    row_energy = jnp.sum(scalar * read_t[:, 0:1] + rounded * read_t[:, 1:2], axis=0, keepdims=True)
    energy[...] = row_energy * live_row(count)
    lanes = iota((SLOTS, LANES), 1)
    eye = (lanes == iota((SLOTS, LANES), 0)).astype(F32).astype(BF16)
    chosen = (iota((EXPORT, LANES), 1) == picked[...]).astype(F32).astype(BF16)
    own_rows[...] = dot_nt(eye, features).astype(BF16)
    outgoing[...] = dot_nt(chosen, features).astype(BF16)


def second_kernel(
    count_ref, table, own_rows, low, mid, high, index, win_t, win, wout_t, wout, mix_t, mix_rest, read,
    grad_own, grad_low, grad_mid, grad_high, pair_out, energy,
    feats, projected, onehot, radial, source, grad_radial, grad_source,
):
    count = count_ref[0]
    ids = index[...]
    unit, inverse, _, basis, basis_slope = geometry(table[...], ids, count, True)
    before, gate = hidden_of(win_t[...], basis)
    hidden = (before * gate).astype(BF16)
    feats[0:SLOTS, :] = own_rows[...]
    feats[SLOTS : SLOTS + SLAB, :] = low[...]
    feats[SLOTS + SLAB : SLOTS + 2 * SLAB, :] = mid[...]
    feats[SLOTS + 2 * SLAB : SLOTS + 3 * SLAB, :] = high[...]
    feats[SLOTS + 3 * SLAB :, :] = jnp.zeros((TABLE - SLOTS - 3 * SLAB, 4 * C), BF16)
    for c in range(4):
        projected[c * C : (c + 1) * C, :] = dot_nt(
            mix_t[min(c, 1)], feats[:, c * C : (c + 1) * C]
        ).astype(BF16)
    entry = iota((TABLE, LANES), 0)
    for m in range(COLUMNS):
        onehot[:, m * LANES : (m + 1) * LANES] = (entry == column(ids, m)).astype(F32).astype(BF16)
    units = [[column(unit[x : x + 1], m) for m in range(COLUMNS)] for x in range(3)]
    wide = 2 * LANES
    a0 = jnp.zeros((C, LANES), F32)
    a1 = [jnp.zeros((C, LANES), F32) for _ in range(3)]
    for w in range(PAIRS // wide):
        at = slice(w * wide, (w + 1) * wide)
        radial[:, at] = dot_nn(wout_t[...], hidden[:, at])
        source[:, at] = dot_nn(projected[...], onehot[:, at])
        for m in (2 * w, 2 * w + 1):
            here = slice(m * LANES, (m + 1) * LANES)
            s = source[0:C, here]
            v = [source[(x + 1) * C : (x + 2) * C, here] for x in range(3)]
            u = [units[x][m] for x in range(3)]
            along = v[0] * u[0] + v[1] * u[1] + v[2] * u[2]
            a0 = a0 + radial[0:C, here] * s + radial[3 * C :, here] * along
            t = radial[C : 2 * C, here] * s
            r3 = radial[2 * C : 3 * C, here]
            for x in range(3):
                a1[x] = a1[x] + t * u[x] + r3 * v[x]
    a0 = fold(a0) * NORM
    a1 = [fold(v) * NORM for v in a1]
    quad = a1[0] * a1[0] + a1[1] * a1[1] + a1[2] * a1[2]
    read_high = read[...].astype(BF16)
    read_low = (read[...] - read_high.astype(F32)).astype(BF16)
    rests = dot_nt(mix_rest[...], read_high) + dot_nt(mix_rest[...], read_low)
    m2, m3, m4 = [rests[k * C : (k + 1) * C, 1:2] for k in range(3)]
    live = live_row(count)
    energy[...] = live * jnp.sum(a0 * m2 + a0 * a0 * m3 + quad * m4, axis=0, keepdims=True)
    live = live * NORM
    d0 = (m2 + 2.0 * a0 * m3) * live
    d1 = [2.0 * v * m4 * live for v in a1]
    grad_units = [[], [], []]
    for m in range(COLUMNS):
        here = slice(m * LANES, (m + 1) * LANES)
        s = source[0:C, here]
        v = [source[(x + 1) * C : (x + 2) * C, here] for x in range(3)]
        u = [units[x][m] for x in range(3)]
        r1, r2, r3, r4 = [radial[k * C : (k + 1) * C, here] for k in range(4)]
        along = v[0] * u[0] + v[1] * u[1] + v[2] * u[2]
        slant = d1[0] * u[0] + d1[1] * u[1] + d1[2] * u[2]
        grad_radial[0:C, here] = (d0 * s).astype(BF16)
        grad_radial[C : 2 * C, here] = (s * slant).astype(BF16)
        grad_radial[2 * C : 3 * C, here] = (d1[0] * v[0] + d1[1] * v[1] + d1[2] * v[2]).astype(BF16)
        grad_radial[3 * C :, here] = (d0 * along).astype(BF16)
        grad_source[0:C, here] = (r1 * d0 + r2 * slant).astype(BF16)
        q = d0 * r4
        t = r2 * s
        for x in range(3):
            grad_source[(x + 1) * C : (x + 2) * C, here] = (q * u[x] + r3 * d1[x]).astype(BF16)
            grad_units[x].append(jnp.sum(q * v[x] + t * d1[x], axis=0, keepdims=True))
    grad_unit = stack_rows([jnp.concatenate(g, axis=1) for g in grad_units])
    grad_hidden = dot_nn(wout[...], grad_radial[...])
    grad_before = (grad_hidden * (gate * (1.0 + before * (1.0 - gate)))).astype(BF16)
    grad_basis = dot_nn(win[...], grad_before)
    grad_distance = jnp.sum(grad_basis * basis_slope, axis=0, keepdims=True)
    pair_out[...] = pair_gradient(unit, inverse, grad_unit, grad_distance)
    grad_projected = dot_nt(onehot[...], grad_source[...])
    outs = (grad_low, grad_mid, grad_high)
    live_rows = (iota((SLOTS, 1), 0) < count).astype(F32)
    for c in range(4):
        at = slice(c * C, (c + 1) * C)
        rows = dot_nn(grad_projected[:, at].astype(BF16), mix_t[min(c, 1)])
        mine = rows[0:SLOTS]
        if c == 0:
            mine = mine + live_rows * read[1:2, :]
        grad_own[:, at] = mine
        for k in range(3):
            begin = SLOTS + k * SLAB
            outs[k][:, at] = rows[begin : begin + SLAB].astype(BF16)


def third_kernel(
    count_ref, table, sums, grad_own, back, picked, pair_in, index, win_t, win, wout_t, wout, mix_rest, spread, read_t,
    grad_mine, grad_low, grad_mid, grad_high,
    onehot, grad_radial,
):
    count = count_ref[0]
    ids = index[...]
    unit, inverse, kind, basis, basis_slope = geometry(table[...], ids, count, True)
    before, gate = hidden_of(win_t[...], basis)
    hidden = (before * gate).astype(BF16)
    species = (iota((16, PAIRS), 0) % 8 == kind.astype(jnp.int32)).astype(F32).astype(BF16)
    entry = iota((TABLE, LANES), 0)
    for m in range(COLUMNS):
        onehot[:, m * LANES : (m + 1) * LANES] = (entry == column(ids, m)).astype(F32).astype(BF16)
    mine = grad_own[...]
    mine_high = mine.astype(BF16)
    mine_low = (mine - mine_high.astype(F32)).astype(BF16)
    came = back[...].astype(F32)
    came_high = came.astype(BF16)
    came_low = (came - came_high.astype(F32)).astype(BF16)
    eye = (iota((SLOTS, LANES), 1) % SLOTS == iota((SLOTS, LANES), 0)).astype(F32).astype(BF16)
    chosen = (iota((EXPORT, LANES), 1) % SLOTS == picked[...]).astype(F32).astype(BF16)
    left = jnp.concatenate([mine_high, mine_low, came_high, came_low], axis=0)
    right = jnp.concatenate([eye, eye, chosen, chosen], axis=0)
    grads = dot_tn(left, right)
    live = live_row(count)
    gs = grads[0:C] + read_t[:, 0:1] * live
    gv = [grads[(x + 1) * C : (x + 2) * C] for x in range(3)]
    a0 = sums[0:C, :]
    a1 = [sums[(x + 1) * C : (x + 2) * C, :] for x in range(3)]
    first = fold(dot_nn(mix_rest[0 : 3 * C, :], halves(gs)))
    others = fold_columns(dot_nn(mix_rest[3 * C : 5 * C, :], jnp.concatenate([halves(g) for g in gv], axis=1)))
    straight = [column(others[0:C], x) for x in range(3)]
    crossed = [column(others[C : 2 * C], x) for x in range(3)]
    scale = live * NORM
    d0 = first[0:C] + 2.0 * a0 * first[C : 2 * C]
    for x in range(3):
        d0 = d0 + a1[x] * crossed[x]
    d0 = d0 * scale
    d1 = [(straight[x] + a0 * crossed[x] + 2.0 * a1[x] * first[2 * C : 3 * C]) * scale for x in range(3)]
    grad_units = [[], [], []]
    for m in range(COLUMNS):
        here = slice(m * LANES, (m + 1) * LANES)
        r2 = dot_nn(wout_t[C : 2 * C, :], column(hidden, m))
        source = dot_nn(spread[...], column(species, m))
        u = [column(unit[x : x + 1], m) for x in range(3)]
        slant = d1[0] * u[0] + d1[1] * u[1] + d1[2] * u[2]
        grad_radial[0:C, here] = (d0 * source).astype(BF16)
        grad_radial[C:, here] = (slant * source).astype(BF16)
        q = r2 * source
        for x in range(3):
            grad_units[x].append(jnp.sum(q * d1[x], axis=0, keepdims=True))
    grad_unit = stack_rows([jnp.concatenate(g, axis=1) for g in grad_units])
    grad_hidden = dot_nn(wout[...], grad_radial[...])
    grad_before = (grad_hidden * (gate * (1.0 + before * (1.0 - gate)))).astype(BF16)
    grad_basis = dot_nn(win[...], grad_before)
    grad_distance = jnp.sum(grad_basis * basis_slope, axis=0, keepdims=True)
    pairs = pair_in[...] + pair_gradient(unit, inverse, grad_unit, grad_distance)
    pair_high = pairs.astype(BF16)
    pair_low = (pairs - pair_high.astype(F32)).astype(BF16)
    both = jnp.concatenate([pair_high.astype(F32), pair_low.astype(F32)], axis=0).astype(BF16)
    spread_back = dot_nt(both, onehot[...])
    grads = spread_back[0:8] + spread_back[8:16]
    total = column(pairs, 0)
    for m in range(1, COLUMNS):
        total = total + column(pairs, m)
    grad_mine[...] = column(grads, 0) - fold(total)
    outs = (grad_low, grad_mid, grad_high)
    for b in range(27):
        at = SLOTS + b * EXPORT
        tile = column(grads, at // LANES)
        offset = at % LANES
        if offset:
            tile = pltpu.roll(tile, LANES - offset, 1)
        outs[b // 9][b % 9] = tile


def fold_columns(values):
    count = values.shape[1] // LANES
    return jnp.concatenate([fold(column(values, x)) for x in range(count)], axis=1)


def last_kernel(exports, count_ref, grad_mine, back, energy_one, energy_two, forces, energies):
    lane = iota((8, LANES), 1)
    total = grad_mine[...]
    came = back[...]
    source = jnp.zeros((8, LANES), jnp.int32)
    hit = jnp.zeros((8, LANES), F32)
    for e in range(EXPORT):
        same = lane == exports[e]
        source = jnp.where(same, e, source)
        hit = jnp.where(same, 1.0, hit)
    total = total + jnp.where(hit > 0.5, jnp.take_along_axis(came, source, axis=1), 0.0)
    forces[...] = -total[0:3, 0:SLOTS]
    energies[...] = (live_row(count_ref[0]) * (energy_one[...] + energy_two[...]))[:, 0:SLOTS]


def call(kernel, outs, specs, scratch=(), limit=None, smem=0):
    count = len(specs)
    in_specs = [pl.BlockSpec(memory_space=pltpu.SMEM)] * smem
    in_specs += [pl.BlockSpec(memory_space=pltpu.VMEM)] * (count - smem)
    many = isinstance(outs, (list, tuple))
    return pl.pallas_call(
        kernel,
        out_shape=[jax.ShapeDtypeStruct(s, t) for s, t in outs],
        in_specs=in_specs,
        out_specs=[pl.BlockSpec(memory_space=pltpu.VMEM)] * len(outs),
        scratch_shapes=[pltpu.VMEM(s, t) for s, t in scratch],
        compiler_params=pltpu.CompilerParams(vmem_limit_bytes=limit or (16 << 20)),
    )(*specs)


def domain(x, y, z):
    return (x % 16 * 4 + y % 4) * 8 + z % 8


def moves(step):
    sx, sy, sz = step
    return [
        (domain(x, y, z), domain(x + sx, y + sy, z + sz))
        for x in range(16)
        for y in range(4)
        for z in range(8)
    ]


UP = ((1, 0, 0), (0, 1, 0), (0, 0, 1))
DOWN = ((-1, 0, 0), (0, -1, 0), (0, 0, -1))


def send(value, step):
    return lax.ppermute(value, AXES, moves(step))


def spread_halo(block):
    for axis in range(2):
        low = send(block, UP[axis])
        high = send(block, DOWN[axis])
        block = jnp.concatenate([low, block, high], axis=0)
    return send(block, UP[2]), block, send(block, DOWN[2])


def gather_halo(low, mid, high):
    for axis in (2, 1, 0):
        from_low = send(high, UP[axis])
        from_high = send(low, DOWN[axis])
        block = mid + from_low + from_high
        if axis:
            third = block.shape[0] // 3
            low, mid, high = block[:third], block[third : 2 * third], block[2 * third :]
    return block


def body(
    positions, species, counts, neighbours, exports, embedding, radial_in,
    radial_out_one, radial_out_two, mix_one, mix_two, readout,
):
    own, payload, picked = call(
        start_kernel,
        [((8, LANES), F32), ((8, LANES), F32), ((EXPORT, LANES), jnp.int32)],
        [exports, positions, species.reshape(1, SLOTS)],
        smem=1,
    )
    block = (neighbours - SLOTS) // EXPORT
    turned = block % 3 * 9 + block // 3 % 3 * 3 + block // 9
    moved = SLOTS + turned * EXPORT + neighbours % EXPORT
    index = jnp.where(neighbours < SLOTS, neighbours, moved).reshape(1, PAIRS)
    emb = jnp.concatenate([embedding, jnp.zeros((1, C), BF16)], axis=0)
    emb_t = emb.T
    win_t = jnp.swapaxes(radial_in, 1, 2)
    one_t = radial_out_one.T
    two_t = radial_out_two.T
    mix0_t = mix_one[0].T
    mix_a = mix_one[1:4].reshape(3 * C, C).T
    mix_b = mix_one[4:6].reshape(2 * C, C).T
    mix_back = mix_one[1:6].reshape(5 * C, C)
    mix_two_t = jnp.swapaxes(mix_two[0:2], 1, 2)
    mix_two_rest = mix_two[2:5].reshape(3 * C, C)
    read_t = readout.T
    read = jnp.concatenate([readout, jnp.zeros((6, C), F32)], axis=0)

    low, mid, high = spread_halo(payload[None])
    table, own_rows, outgoing, sums, energy_one, spread = call(
        lambda *refs: first_kernel(*refs, None),
        [
            ((8, TABLE), F32),
            ((SLOTS, 4 * C), BF16),
            ((EXPORT, 4 * C), BF16),
            ((4 * C, LANES), F32),
            ((1, LANES), F32),
            ((C, 16), BF16),
        ],
        [counts, own, low, mid, high, index, picked, win_t[0], one_t, mix_a, mix_b, mix0_t, emb, emb_t, read_t],
        smem=1,
    )
    low, mid, high = spread_halo(outgoing)
    grad_own, grad_low, grad_mid, grad_high, pairs, energy_two = call(
        second_kernel,
        [
            ((SLOTS, 4 * C), F32),
            ((SLAB, 4 * C), BF16),
            ((SLAB, 4 * C), BF16),
            ((SLAB, 4 * C), BF16),
            ((8, PAIRS), F32),
            ((1, LANES), F32),
        ],
        [
            counts, table, own_rows, low, mid, high, index, win_t[1], radial_in[1], two_t, radial_out_two,
            mix_two_t, mix_two_rest, read,
        ],
        scratch=[
            ((TABLE, 4 * C), BF16),
            ((4 * C, TABLE), BF16),
            ((TABLE, PAIRS), BF16),
            ((4 * C, PAIRS), F32),
            ((4 * C, PAIRS), F32),
            ((4 * C, PAIRS), BF16),
            ((4 * C, PAIRS), BF16),
        ],
        limit=48 << 20,
        smem=1,
    )
    back = gather_halo(grad_low, grad_mid, grad_high)
    grad_mine, grad_low, grad_mid, grad_high = call(
        third_kernel,
        [((8, LANES), F32), ((9, 8, LANES), F32), ((9, 8, LANES), F32), ((9, 8, LANES), F32)],
        [
            counts, table, sums, grad_own, back, picked, pairs, index, win_t[0], radial_in[0], one_t,
            radial_out_one, mix_back, spread, read_t,
        ],
        scratch=[((TABLE, PAIRS), BF16), ((2 * C, PAIRS), BF16)],
        limit=32 << 20,
        smem=1,
    )
    back = gather_halo(grad_low, grad_mid, grad_high)
    forces, energies = call(
        last_kernel,
        [((3, SLOTS), F32), ((1, SLOTS), F32)],
        [exports, counts, grad_mine, back[0], energy_one, energy_two],
        smem=2,
    )
    return forces, energies.reshape(SLOTS)


def solution(mesh):
    whole = P()
    split = P(AXES)
    in_specs = (P(None, AXES), split, split, P(None, AXES), split) + (whole,) * 7
    out_specs = (P(None, AXES), split)
    return jax.shard_map(body, mesh=mesh, in_specs=in_specs, out_specs=out_specs, check_vma=False)
```

```python
import math

import jax
import jax.numpy as jnp
from jax import lax
from jax.experimental import pallas as pl
from jax.experimental.pallas import tpu as pltpu
from jax.sharding import PartitionSpec as P

C = 128
NB = 8
RH = 64
NSPEC = 7
SLOTS = 64
DEPTH = 32
EXPORT = 16
PAIRS = SLOTS * DEPTH
SLAB = 9 * EXPORT
TABLE = 512
LANES = 128
COLUMNS = PAIRS // LANES
DOMAIN_LENGTH = 6.0
CUTOFF = 6.0
SOFTEN = 0.25
NORM = 1.0 / math.sqrt(DEPTH)
AXES = ("gx", "gy", "gz")
F32 = jnp.float32
BF16 = jnp.bfloat16


def dot_nn(a, b):
    return lax.dot_general(a, b, (((1,), (0,)), ((), ())), preferred_element_type=F32)


def dot_nt(a, b):
    return lax.dot_general(a, b, (((1,), (1,)), ((), ())), preferred_element_type=F32)


def dot_tn(a, b):
    return lax.dot_general(a, b, (((0,), (0,)), ((), ())), preferred_element_type=F32)


def iota(shape, dim):
    return lax.broadcasted_iota(jnp.int32, shape, dim)


def column(values, m):
    return values[:, m * LANES : (m + 1) * LANES]


def halves(values):
    high = values.astype(BF16)
    low = (values - high.astype(F32)).astype(BF16)
    return jnp.where(iota(values.shape, 1) % LANES < SLOTS, high.astype(F32), low.astype(F32)).astype(BF16)


def fold(values):
    return values + pltpu.roll(values, SLOTS, 1)


def live_row(count):
    return (iota((1, LANES), 1) % SLOTS < count).astype(F32)


def gather_entries(table, index):
    parts = []
    for m in range(COLUMNS):
        ids = jnp.broadcast_to(column(index, m), (8, LANES))
        low = ids & (LANES - 1)
        high = ids >> 7
        found = jnp.take_along_axis(column(table, 0), low, axis=1)
        for v in range(1, TABLE // LANES):
            found = jnp.where(high == v, jnp.take_along_axis(column(table, v), low, axis=1), found)
        parts.append(found)
    return jnp.concatenate(parts, axis=1)


def sincos_pi(turns):
    whole = jnp.floor(turns + 0.5)
    part = turns - whole
    sign = 1.0 - 2.0 * (whole - 2.0 * jnp.floor(whole * 0.5))
    square = part * part
    sine = 0.0
    cosine = 0.0
    for n in range(6, -1, -1):
        cosine = cosine * square + (-1.0) ** n * math.pi ** (2 * n) / math.factorial(2 * n)
    for n in range(5, -1, -1):
        sine = sine * square + (-1.0) ** n * math.pi ** (2 * n + 1) / math.factorial(2 * n + 1)
    return sine * part * sign, cosine * sign


def geometry(table, index, count, with_slope):
    found = gather_entries(table, index)
    first = column(table, 0)
    centre = jnp.where(iota((8, LANES), 1) < SLOTS, first, pltpu.roll(first, SLOTS, 1))
    centre = jnp.concatenate([centre] * COLUMNS, axis=1)
    rows = iota((8, PAIRS), 0)
    delta = jnp.where(rows < 3, found - centre, 0.0)
    kind = found[3:4, :]
    square = jnp.sum(delta * delta, axis=0, keepdims=True) + SOFTEN
    inverse = lax.rsqrt(square)
    distance = square * inverse
    unit = delta * inverse
    slot = iota((1, PAIRS), 1) % SLOTS
    paired = jnp.where(index != slot, jnp.concatenate([live_row(count)] * COLUMNS, axis=1), 0.0)
    scaled = jnp.minimum(distance * (1.0 / CUTOFF), 1.0)
    power = scaled * scaled * scaled
    power = power * power
    envelope = 1.0 + power * (-28.0 + scaled * (48.0 - 21.0 * scaled))
    orders = (iota((8, 1), 0) + 1).astype(F32)
    sine, cosine = sincos_pi(orders * scaled)
    weight = envelope * paired * inverse
    basis = (sine * weight).astype(BF16)
    if not with_slope:
        return unit, inverse, kind, basis, None
    rest = 1.0 - scaled
    slope = (-168.0 / CUTOFF) * (power * rest * rest) / jnp.maximum(scaled, 1e-3)
    basis_slope = weight * cosine * (orders * (math.pi / CUTOFF)) + sine * (
        slope * paired * inverse - weight * inverse
    )
    return unit, inverse, kind, basis, basis_slope


def split(values):
    high = values.astype(BF16)
    return high, (values - high.astype(F32)).astype(BF16)


def keep(values):
    return values.astype(BF16).astype(F32)


def grad_distance_of(wout, win, grad_radial, before, gate, basis_slope):
    half = grad_radial.shape[0] // 2
    grad_hidden = keep(dot_nn(wout[...], grad_radial[0:half, :]) + dot_nn(wout[...], grad_radial[half:, :]))
    high, low = split(grad_hidden * (gate * (1.0 + before * (1.0 - gate))))
    grad_basis = keep(dot_nn(win[...], high) + dot_nn(win[...], low))
    return jnp.sum(grad_basis * basis_slope, axis=0, keepdims=True)


def hidden_of(weights, basis):
    before = dot_nn(weights, basis)
    gate = 1.0 / (1.0 + jnp.exp(-before))
    return before, gate


def pair_gradient(unit, inverse, grad_unit, grad_distance):
    along = jnp.sum(grad_unit * unit, axis=0, keepdims=True)
    return inverse * (grad_unit - unit * along) + unit * grad_distance


def stack_rows(rows):
    where = iota((8, rows[0].shape[1]), 0)
    out = jnp.zeros((8, rows[0].shape[1]), F32)
    for r, row in enumerate(rows):
        out = jnp.where(where == r, row, out)
    return out


def start_kernel(arrived, own, payload, picked, index, count):
    own[...] = jnp.zeros_like(own)
    own[0:4, 0:SLOTS] = arrived[COLUMNS : COLUMNS + 4, 0:SLOTS]
    exports = arrived[COLUMNS + 4 : COLUMNS + 5, :]
    count[...] = arrived[COLUMNS + 5 : COLUMNS + 6, :].astype(jnp.int32)
    mine = iota((EXPORT, LANES), 1) == iota((EXPORT, LANES), 0)
    pick = jnp.sum(jnp.where(mine, exports, 0.0), axis=1, keepdims=True)
    picked[...] = jnp.broadcast_to(pick, (EXPORT, LANES)).astype(jnp.int32)
    source = jnp.broadcast_to(exports, (8, LANES)).astype(jnp.int32)
    payload[...] = jnp.take_along_axis(own[...], source, axis=1)
    for m in range(COLUMNS):
        index[:, m * LANES : (m + 1) * LANES] = arrived[m : m + 1, :].astype(jnp.int32)


def first_kernel(
    count_ref, own, low, mid, high, index, picked, win_t, wout_t, mix_a, mix_b, mix0_t, emb, emb_t, read_t,
    table, own_rows, outgoing, sums, energy, spread, radial,
):
    count = count_ref[...]
    group = iota((8, LANES), 1) // EXPORT
    rows8 = iota((8, 1), 0)
    tiles = [own[...]] + [jnp.zeros((8, LANES), F32) for _ in range(3)]
    slabs = (low, mid, high)
    for b in range(27):
        oz, oy, ox = b // 9 - 1, b // 3 % 3 - 1, b % 3 - 1
        entry = SLOTS + b * EXPORT
        shift = jnp.where(rows8 == 0, DOMAIN_LENGTH * ox, 0.0)
        shift = jnp.where(rows8 == 1, DOMAIN_LENGTH * oy, shift)
        shift = jnp.where(rows8 == 2, DOMAIN_LENGTH * oz, shift)
        tile = entry // LANES
        at = entry % LANES // EXPORT
        tiles[tile] = jnp.where(group == at, slabs[oz + 1][b % 9] + shift, tiles[tile])
    for v in range(4):
        table[:, v * LANES : (v + 1) * LANES] = tiles[v]
    whole = jnp.concatenate(tiles, axis=1)
    ids = index[...]
    unit, inverse, kind, basis, _ = geometry(whole, ids, count, False)
    before, gate = hidden_of(win_t[...], basis)
    hidden = (before * gate).astype(BF16)
    pe = dot_nt(mix0_t[...], emb[...])
    pe_high = pe.astype(BF16)
    pe_low = (pe - pe_high.astype(F32)).astype(BF16)
    pe_both = jnp.concatenate([pe_high.astype(F32), pe_low.astype(F32)], axis=1).astype(BF16)
    spread[...] = pe_both
    species = (iota((16, PAIRS), 0) % 8 == kind.astype(jnp.int32)).astype(F32).astype(BF16)
    a0 = jnp.zeros((C, LANES), F32)
    a1 = [jnp.zeros((C, LANES), F32) for _ in range(3)]
    for m in range(COLUMNS):
        radial = dot_nn(wout_t[...], column(hidden, m))
        source = dot_nn(pe_both, column(species, m))
        a0 = a0 + radial[:C] * source
        t = radial[C:] * source
        for x in range(3):
            a1[x] = a1[x] + t * column(unit[x : x + 1], m)
    a0 = fold(a0) * NORM
    a1 = [fold(v) * NORM for v in a1]
    for x, v in enumerate([a0] + a1):
        sums[x * C : (x + 1) * C, :] = v
    quad = a1[0] * a1[0] + a1[1] * a1[1] + a1[2] * a1[2]
    own_kind = (iota((8, LANES), 0) == whole[3:4, :LANES].astype(jnp.int32)).astype(F32).astype(BF16)
    own_kind = jnp.where(iota((8, LANES), 1) < SLOTS, own_kind.astype(F32), 0.0).astype(BF16)
    scalar = dot_nn(emb_t[...], own_kind)
    scalar = scalar + dot_nn(mix_a[...], jnp.concatenate([halves(a0), halves(a0 * a0), halves(quad)], axis=0))
    scalar = fold(scalar)
    top = jnp.concatenate([halves(v) for v in a1], axis=1)
    bottom = jnp.concatenate([halves(a0 * v) for v in a1], axis=1)
    vector = dot_nn(mix_b[...], jnp.concatenate([top, bottom], axis=0))
    parts = [scalar] + [fold(column(vector, x)) for x in range(3)]
    features = jnp.concatenate(parts, axis=0).astype(BF16)
    rounded = features[:C].astype(F32)
    row_energy = jnp.sum(scalar * read_t[:, 0:1] + rounded * read_t[:, 1:2], axis=0, keepdims=True)
    energy[...] = row_energy * live_row(count)
    lanes = iota((SLOTS, LANES), 1)
    eye = (lanes == iota((SLOTS, LANES), 0)).astype(F32).astype(BF16)
    chosen = (iota((EXPORT, LANES), 1) == picked[...]).astype(F32).astype(BF16)
    own_rows[...] = dot_nt(eye, features).astype(BF16)
    outgoing[...] = dot_nt(chosen, features).astype(BF16)


def second_kernel(
    count_ref, table, own_rows, low, mid, high, index, win_t, win, wout_t, wout, mix_t, mix_rest, read,
    grad_own, grad_low, grad_mid, grad_high, pair_out, energy,
    feats, turned, onehot, radial, source, grad_radial, grad_source,
):
    count = count_ref[...]
    ids = index[...]
    unit, inverse, _, basis, basis_slope = geometry(table[...], ids, count, True)
    before, gate = hidden_of(win_t[...], basis)
    hidden = (before * gate).astype(BF16)
    feats[0:SLOTS, :] = own_rows[...]
    feats[SLOTS : SLOTS + SLAB, :] = low[...]
    feats[SLOTS + SLAB : SLOTS + 2 * SLAB, :] = mid[...]
    feats[SLOTS + 2 * SLAB : SLOTS + 3 * SLAB, :] = high[...]
    feats[SLOTS + 3 * SLAB :, :] = jnp.zeros((TABLE - SLOTS - 3 * SLAB, 4 * C), BF16)
    eye = (iota((C, C), 0) == iota((C, C), 1)).astype(F32).astype(BF16)
    for c in range(4):
        turned[c * C : (c + 1) * C, :] = dot_nt(eye, feats[:, c * C : (c + 1) * C]).astype(BF16)
    entry = iota((TABLE, LANES), 0)
    for m in range(COLUMNS):
        onehot[:, m * LANES : (m + 1) * LANES] = (entry == column(ids, m)).astype(F32).astype(BF16)
    units = [[column(unit[x : x + 1], m) for m in range(COLUMNS)] for x in range(3)]
    wide = 2 * LANES
    a0 = jnp.zeros((C, LANES), F32)
    a1 = [jnp.zeros((C, LANES), F32) for _ in range(3)]
    for w in range(PAIRS // wide):
        at = slice(w * wide, (w + 1) * wide)
        radial[:, at] = dot_nn(wout_t[...], hidden[:, at])
        picked = dot_nn(turned[...], onehot[:, at]).astype(BF16)
        for c in range(4):
            source[c * C : (c + 1) * C, at] = dot_nn(mix_t[min(c, 1)], picked[c * C : (c + 1) * C])
        for m in (2 * w, 2 * w + 1):
            here = slice(m * LANES, (m + 1) * LANES)
            s = source[0:C, here]
            v = [source[(x + 1) * C : (x + 2) * C, here] for x in range(3)]
            u = [units[x][m] for x in range(3)]
            along = v[0] * u[0] + v[1] * u[1] + v[2] * u[2]
            a0 = a0 + radial[0:C, here] * s + radial[3 * C :, here] * along
            t = radial[C : 2 * C, here] * s
            r3 = radial[2 * C : 3 * C, here]
            for x in range(3):
                a1[x] = a1[x] + t * u[x] + r3 * v[x]
    a0 = fold(a0) * NORM
    a1 = [fold(v) * NORM for v in a1]
    quad = a1[0] * a1[0] + a1[1] * a1[1] + a1[2] * a1[2]
    read_high = read[...].astype(BF16)
    read_low = (read[...] - read_high.astype(F32)).astype(BF16)
    rests = dot_nt(mix_rest[...], read_high) + dot_nt(mix_rest[...], read_low)
    m2, m3, m4 = [rests[k * C : (k + 1) * C, 1:2] for k in range(3)]
    live = live_row(count)
    energy[...] = live * jnp.sum(a0 * m2 + a0 * a0 * m3 + quad * m4, axis=0, keepdims=True)
    live = live * NORM
    d0 = (m2 + 2.0 * a0 * m3) * live
    d1 = [2.0 * v * m4 * live for v in a1]
    grad_units = [[], [], []]
    for m in range(COLUMNS):
        here = slice(m * LANES, (m + 1) * LANES)
        s = source[0:C, here]
        v = [source[(x + 1) * C : (x + 2) * C, here] for x in range(3)]
        u = [units[x][m] for x in range(3)]
        r1, r2, r3, r4 = [radial[k * C : (k + 1) * C, here] for k in range(4)]
        along = v[0] * u[0] + v[1] * u[1] + v[2] * u[2]
        slant = d1[0] * u[0] + d1[1] * u[1] + d1[2] * u[2]
        parts = (d0 * s, s * slant, d1[0] * v[0] + d1[1] * v[1] + d1[2] * v[2], d0 * along)
        for k in range(4):
            high_part, low_part = split(parts[k])
            grad_radial[k * C : (k + 1) * C, here] = high_part
            grad_radial[(k + 4) * C : (k + 5) * C, here] = low_part
        grad_source[0:C, here] = (r1 * d0 + r2 * slant).astype(BF16)
        q = d0 * r4
        t = r2 * s
        for x in range(3):
            grad_source[(x + 1) * C : (x + 2) * C, here] = (q * u[x] + r3 * d1[x]).astype(BF16)
            grad_units[x].append(jnp.sum(q * v[x] + t * d1[x], axis=0, keepdims=True))
    grad_unit = stack_rows([jnp.concatenate(g, axis=1) for g in grad_units])
    grad_distance = grad_distance_of(wout, win, grad_radial, before, gate, basis_slope)
    pair_out[...] = pair_gradient(unit, inverse, grad_unit, grad_distance)
    grad_projected = dot_nt(onehot[...], grad_source[...])
    outs = (grad_low, grad_mid, grad_high)
    live_rows = (iota((SLOTS, 1), 0) < count[:, 0:1]).astype(F32)
    for c in range(4):
        at = slice(c * C, (c + 1) * C)
        high_part, low_part = split(grad_projected[:, at])
        rows = dot_nn(high_part, mix_t[min(c, 1)]) + dot_nn(low_part, mix_t[min(c, 1)])
        mine = rows[0:SLOTS]
        if c == 0:
            mine = mine + live_rows * read[1:2, :]
        grad_own[:, at] = mine
        for k in range(3):
            begin = SLOTS + k * SLAB
            outs[k][:, at] = rows[begin : begin + SLAB].astype(BF16)


def third_kernel(
    count_ref, table, sums, grad_own, back, picked, pair_in, index, win_t, win, wout_t, wout, mix_rest, spread, read_t,
    grad_mine, grad_low, grad_mid, grad_high,
    onehot, grad_radial,
):
    count = count_ref[...]
    ids = index[...]
    unit, inverse, kind, basis, basis_slope = geometry(table[...], ids, count, True)
    before, gate = hidden_of(win_t[...], basis)
    hidden = (before * gate).astype(BF16)
    species = (iota((16, PAIRS), 0) % 8 == kind.astype(jnp.int32)).astype(F32).astype(BF16)
    entry = iota((TABLE, LANES), 0)
    for m in range(COLUMNS):
        onehot[:, m * LANES : (m + 1) * LANES] = (entry == column(ids, m)).astype(F32).astype(BF16)
    mine = grad_own[...]
    mine_high = mine.astype(BF16)
    mine_low = (mine - mine_high.astype(F32)).astype(BF16)
    came = back[...].astype(F32)
    came_high = came.astype(BF16)
    came_low = (came - came_high.astype(F32)).astype(BF16)
    eye = (iota((SLOTS, LANES), 1) % SLOTS == iota((SLOTS, LANES), 0)).astype(F32).astype(BF16)
    chosen = (iota((EXPORT, LANES), 1) % SLOTS == picked[...]).astype(F32).astype(BF16)
    left = jnp.concatenate([mine_high, mine_low, came_high, came_low], axis=0)
    right = jnp.concatenate([eye, eye, chosen, chosen], axis=0)
    grads = dot_tn(left, right)
    live = live_row(count)
    gs = grads[0:C] + read_t[:, 0:1] * live
    gv = [grads[(x + 1) * C : (x + 2) * C] for x in range(3)]
    a0 = sums[0:C, :]
    a1 = [sums[(x + 1) * C : (x + 2) * C, :] for x in range(3)]
    first = fold(dot_nn(mix_rest[0 : 3 * C, :], halves(gs)))
    others = fold_columns(dot_nn(mix_rest[3 * C : 5 * C, :], jnp.concatenate([halves(g) for g in gv], axis=1)))
    straight = [column(others[0:C], x) for x in range(3)]
    crossed = [column(others[C : 2 * C], x) for x in range(3)]
    scale = live * NORM
    d0 = first[0:C] + 2.0 * a0 * first[C : 2 * C]
    for x in range(3):
        d0 = d0 + a1[x] * crossed[x]
    d0 = d0 * scale
    d1 = [(straight[x] + a0 * crossed[x] + 2.0 * a1[x] * first[2 * C : 3 * C]) * scale for x in range(3)]
    grad_units = [[], [], []]
    for m in range(COLUMNS):
        here = slice(m * LANES, (m + 1) * LANES)
        r2 = dot_nn(wout_t[C : 2 * C, :], column(hidden, m))
        source = dot_nn(spread[...], column(species, m))
        u = [column(unit[x : x + 1], m) for x in range(3)]
        slant = d1[0] * u[0] + d1[1] * u[1] + d1[2] * u[2]
        parts = (d0 * source, slant * source)
        for k in range(2):
            high_part, low_part = split(parts[k])
            grad_radial[k * C : (k + 1) * C, here] = high_part
            grad_radial[(k + 2) * C : (k + 3) * C, here] = low_part
        q = r2 * source
        for x in range(3):
            grad_units[x].append(jnp.sum(q * d1[x], axis=0, keepdims=True))
    grad_unit = stack_rows([jnp.concatenate(g, axis=1) for g in grad_units])
    grad_distance = grad_distance_of(wout, win, grad_radial, before, gate, basis_slope)
    pairs = pair_in[...] + pair_gradient(unit, inverse, grad_unit, grad_distance)
    pair_high = pairs.astype(BF16)
    pair_low = (pairs - pair_high.astype(F32)).astype(BF16)
    both = jnp.concatenate([pair_high.astype(F32), pair_low.astype(F32)], axis=0).astype(BF16)
    spread_back = dot_nt(both, onehot[...])
    grads = spread_back[0:8] + spread_back[8:16]
    total = column(pairs, 0)
    for m in range(1, COLUMNS):
        total = total + column(pairs, m)
    grad_mine[...] = column(grads, 0) - fold(total)
    outs = (grad_low, grad_mid, grad_high)
    for b in range(27):
        at = SLOTS + b * EXPORT
        tile = column(grads, at // LANES)
        offset = at % LANES
        if offset:
            tile = pltpu.roll(tile, LANES - offset, 1)
        outs[b // 9][b % 9] = tile


def fold_columns(values):
    count = values.shape[1] // LANES
    return jnp.concatenate([fold(column(values, x)) for x in range(count)], axis=1)


def last_kernel(count_ref, grad_mine, back, picked, energy_one, energy_two, out):
    same = iota((EXPORT, LANES), 1) == picked[...]
    entry = jnp.sum(jnp.where(same, iota((EXPORT, LANES), 0), 0), axis=0, keepdims=True)
    hit = jnp.sum(same.astype(F32), axis=0, keepdims=True)
    came = jnp.take_along_axis(back[...], jnp.broadcast_to(entry, (8, LANES)), axis=1)
    forces = -(grad_mine[...] + came * hit)
    energies = live_row(count_ref[...]) * (energy_one[...] + energy_two[...])
    out[...] = jnp.where(iota((8, LANES), 0) == 3, energies, forces)


def call(kernel, outs, specs, scratch=(), limit=None):
    return pl.pallas_call(
        kernel,
        out_shape=[jax.ShapeDtypeStruct(s, t) for s, t in outs],
        in_specs=[pl.BlockSpec(memory_space=pltpu.VMEM)] * len(specs),
        out_specs=[pl.BlockSpec(memory_space=pltpu.VMEM)] * len(outs),
        scratch_shapes=[pltpu.VMEM(s, t) for s, t in scratch],
        compiler_params=pltpu.CompilerParams(vmem_limit_bytes=limit or (16 << 20)),
    )(*specs)


DOMAINS = [(x, y, z) for x in range(16) for y in range(4) for z in range(8)]


def given(x, y, z):
    return (x * 4 + y) * 8 + z


def seat(x, y, z):
    x, y, z = x % 16, y % 4, z % 8
    return given(z // 2 * 4 + x // 8 * 2 + z % 2, y, x % 8)


MOVE_IN = [(given(*d), seat(*d)) for d in DOMAINS]
MOVE_OUT = [(there, here) for here, there in MOVE_IN]


def moves(step):
    return [(seat(*d), seat(*(a + b for a, b in zip(d, step)))) for d in DOMAINS]


UP = ((1, 0, 0), (0, 1, 0), (0, 0, 1))
DOWN = ((-1, 0, 0), (0, -1, 0), (0, 0, -1))


def send(value, step):
    return lax.ppermute(value, AXES, moves(step))


def spread_halo(block):
    for axis in range(2):
        low = send(block, UP[axis])
        high = send(block, DOWN[axis])
        block = jnp.concatenate([low, block, high], axis=0)
    return send(block, UP[2]), block, send(block, DOWN[2])


def gather_halo(low, mid, high):
    for axis in (2, 1, 0):
        from_low = send(high, UP[axis])
        from_high = send(low, DOWN[axis])
        block = mid + from_low + from_high
        if axis:
            third = block.shape[0] // 3
            low, mid, high = block[:third], block[third : 2 * third], block[2 * third :]
    return block


def body(
    positions, species, counts, neighbours, exports, embedding, radial_in,
    radial_out_one, radial_out_two, mix_one, mix_two, readout,
):
    block = (neighbours - SLOTS) // EXPORT
    turned = block % 3 * 9 + block // 3 % 3 * 3 + block // 9
    moved = SLOTS + turned * EXPORT + neighbours % EXPORT
    moved = jnp.where(neighbours < SLOTS, neighbours, moved).astype(F32)
    slots = jnp.concatenate([positions, species.astype(F32)[None]], axis=0)
    packed = jnp.concatenate(
        [
            moved.reshape(COLUMNS, LANES),
            jnp.pad(slots, ((0, 0), (0, LANES - SLOTS))),
            jnp.tile(exports.astype(F32), LANES // EXPORT)[None],
            jnp.broadcast_to(counts.astype(F32)[None], (1, LANES)),
            jnp.zeros((2, LANES), F32),
        ],
        axis=0,
    )
    arrived = lax.ppermute(packed, AXES, MOVE_IN)
    own, payload, picked, index, count = call(
        start_kernel,
        [
            ((8, LANES), F32),
            ((8, LANES), F32),
            ((EXPORT, LANES), jnp.int32),
            ((1, PAIRS), jnp.int32),
            ((1, LANES), jnp.int32),
        ],
        [arrived],
    )
    emb = jnp.concatenate([embedding, jnp.zeros((1, C), BF16)], axis=0)
    emb_t = emb.T
    win_t = jnp.swapaxes(radial_in, 1, 2)
    one_t = radial_out_one.T
    two_t = radial_out_two.T
    mix0_t = mix_one[0].T
    mix_a = mix_one[1:4].reshape(3 * C, C).T
    mix_b = mix_one[4:6].reshape(2 * C, C).T
    mix_back = mix_one[1:6].reshape(5 * C, C)
    mix_two_t = jnp.swapaxes(mix_two[0:2], 1, 2)
    mix_two_rest = mix_two[2:5].reshape(3 * C, C)
    read_t = readout.T
    read = jnp.concatenate([readout, jnp.zeros((6, C), F32)], axis=0)

    low, mid, high = spread_halo(payload[None])
    table, own_rows, outgoing, sums, energy_one, spread = call(
        lambda *refs: first_kernel(*refs, None),
        [
            ((8, TABLE), F32),
            ((SLOTS, 4 * C), BF16),
            ((EXPORT, 4 * C), BF16),
            ((4 * C, LANES), F32),
            ((1, LANES), F32),
            ((C, 16), BF16),
        ],
        [count, own, low, mid, high, index, picked, win_t[0], one_t, mix_a, mix_b, mix0_t, emb, emb_t, read_t],
    )
    low, mid, high = spread_halo(outgoing)
    grad_own, grad_low, grad_mid, grad_high, pairs, energy_two = call(
        second_kernel,
        [
            ((SLOTS, 4 * C), F32),
            ((SLAB, 4 * C), BF16),
            ((SLAB, 4 * C), BF16),
            ((SLAB, 4 * C), BF16),
            ((8, PAIRS), F32),
            ((1, LANES), F32),
        ],
        [
            count, table, own_rows, low, mid, high, index, win_t[1], radial_in[1], two_t, radial_out_two,
            mix_two_t, mix_two_rest, read,
        ],
        scratch=[
            ((TABLE, 4 * C), BF16),
            ((4 * C, TABLE), BF16),
            ((TABLE, PAIRS), BF16),
            ((4 * C, PAIRS), F32),
            ((4 * C, PAIRS), F32),
            ((8 * C, PAIRS), BF16),
            ((4 * C, PAIRS), BF16),
        ],
        limit=48 << 20,
    )
    back = gather_halo(grad_low, grad_mid, grad_high)
    grad_mine, grad_low, grad_mid, grad_high = call(
        third_kernel,
        [((8, LANES), F32), ((9, 8, LANES), F32), ((9, 8, LANES), F32), ((9, 8, LANES), F32)],
        [
            count, table, sums, grad_own, back, picked, pairs, index, win_t[0], radial_in[0], one_t,
            radial_out_one, mix_back, spread, read_t,
        ],
        scratch=[((TABLE, PAIRS), BF16), ((4 * C, PAIRS), BF16)],
        limit=32 << 20,
    )
    back = gather_halo(grad_low, grad_mid, grad_high)
    (out,) = call(
        last_kernel,
        [((8, LANES), F32)],
        [count, grad_mine, back[0], picked, energy_one, energy_two],
    )
    out = lax.ppermute(out, AXES, MOVE_OUT)
    return out[0:3, 0:SLOTS], out[3, 0:SLOTS]


def solution(mesh):
    whole = P()
    split = P(AXES)
    in_specs = (P(None, AXES), split, split, P(None, AXES), split) + (whole,) * 7
    out_specs = (P(None, AXES), split)
    return jax.shard_map(body, mesh=mesh, in_specs=in_specs, out_specs=out_specs, check_vma=False)
```

```python
import math

import jax
import jax.numpy as jnp
from jax import lax
from jax.experimental import pallas as pl
from jax.experimental.pallas import tpu as pltpu
from jax.sharding import PartitionSpec as P

C = 128
NB = 8
RH = 64
NSPEC = 7
SLOTS = 64
DEPTH = 32
EXPORT = 16
PAIRS = SLOTS * DEPTH
SLAB = 9 * EXPORT
TABLE = 512
LANES = 128
COLUMNS = PAIRS // LANES
DOMAIN_LENGTH = 6.0
CUTOFF = 6.0
SOFTEN = 0.25
NORM = 1.0 / math.sqrt(DEPTH)
AXES = ("gx", "gy", "gz")
F32 = jnp.float32
BF16 = jnp.bfloat16


def dot_nn(a, b):
    return lax.dot_general(a, b, (((1,), (0,)), ((), ())), preferred_element_type=F32)


def dot_nt(a, b):
    return lax.dot_general(a, b, (((1,), (1,)), ((), ())), preferred_element_type=F32)


def dot_tn(a, b):
    return lax.dot_general(a, b, (((0,), (0,)), ((), ())), preferred_element_type=F32)


def iota(shape, dim):
    return lax.broadcasted_iota(jnp.int32, shape, dim)


def column(values, m):
    return values[:, m * LANES : (m + 1) * LANES]


def halves(values):
    high = values.astype(BF16)
    low = (values - high.astype(F32)).astype(BF16)
    return jnp.where(iota(values.shape, 1) % LANES < SLOTS, high.astype(F32), low.astype(F32)).astype(BF16)


def fold(values):
    return values + pltpu.roll(values, SLOTS, 1)


def live_row(count):
    return (iota((1, LANES), 1) % SLOTS < count).astype(F32)


def gather_entries(table, index):
    parts = []
    for m in range(COLUMNS):
        ids = jnp.broadcast_to(column(index, m), (8, LANES))
        low = ids & (LANES - 1)
        high = ids >> 7
        found = jnp.take_along_axis(column(table, 0), low, axis=1)
        for v in range(1, TABLE // LANES):
            found = jnp.where(high == v, jnp.take_along_axis(column(table, v), low, axis=1), found)
        parts.append(found)
    return jnp.concatenate(parts, axis=1)


def sincos_pi(turns):
    whole = jnp.floor(turns + 0.5)
    part = turns - whole
    sign = 1.0 - 2.0 * (whole - 2.0 * jnp.floor(whole * 0.5))
    square = part * part
    sine = 0.0
    cosine = 0.0
    for n in range(6, -1, -1):
        cosine = cosine * square + (-1.0) ** n * math.pi ** (2 * n) / math.factorial(2 * n)
    for n in range(5, -1, -1):
        sine = sine * square + (-1.0) ** n * math.pi ** (2 * n + 1) / math.factorial(2 * n + 1)
    return sine * part * sign, cosine * sign


def geometry(table, index, count):
    found = gather_entries(table, index)
    first = column(table, 0)
    centre = jnp.where(iota((8, LANES), 1) < SLOTS, first, pltpu.roll(first, SLOTS, 1))
    centre = jnp.concatenate([centre] * COLUMNS, axis=1)
    rows = iota((8, PAIRS), 0)
    delta = jnp.where(rows < 3, found - centre, 0.0)
    square = jnp.sum(delta * delta, axis=0, keepdims=True) + SOFTEN
    inverse = lax.rsqrt(square)
    distance = square * inverse
    slot = iota((1, PAIRS), 1) % SLOTS
    paired = jnp.where(index != slot, jnp.concatenate([live_row(count)] * COLUMNS, axis=1), 0.0)
    scaled = jnp.minimum(distance * (1.0 / CUTOFF), 1.0)
    power = scaled * scaled * scaled
    power = power * power
    envelope = 1.0 + power * (-28.0 + scaled * (48.0 - 21.0 * scaled))
    orders = (iota((8, 1), 0) + 1).astype(F32)
    sine, cosine = sincos_pi(orders * scaled)
    weight = envelope * paired * inverse
    basis = (sine * weight).astype(BF16)
    rest = 1.0 - scaled
    slope = (-168.0 / CUTOFF) * (power * rest * rest) / jnp.maximum(scaled, 1e-3)
    basis_slope = weight * cosine * (orders * (math.pi / CUTOFF)) + sine * (
        slope * paired * inverse - weight * inverse
    )
    facts = jnp.where(rows == 3, inverse, jnp.where(rows == 4, found[3:4, :], delta * inverse))
    return facts, basis, basis_slope


def unit_of(facts):
    return jnp.where(iota((8, PAIRS), 0) < 3, facts, 0.0)


def species_of(facts):
    return (iota((16, PAIRS), 0) % 8 == facts[4:5, :].astype(jnp.int32)).astype(F32).astype(BF16)


def split(values):
    high = values.astype(BF16)
    return high, (values - high.astype(F32)).astype(BF16)


def keep(values):
    return values.astype(BF16).astype(F32)


def grad_distance_of(wout, win, grad_radial, before, gate, basis_slope):
    half = grad_radial.shape[0] // 2
    grad_hidden = keep(dot_nn(wout[...], grad_radial[0:half, :]) + dot_nn(wout[...], grad_radial[half:, :]))
    high, low = split(grad_hidden * (gate * (1.0 + before * (1.0 - gate))))
    grad_basis = keep(dot_nn(win, high) + dot_nn(win, low))
    return jnp.sum(grad_basis * basis_slope, axis=0, keepdims=True)


def hidden_of(weights, basis):
    before = dot_nn(weights, basis)
    gate = 1.0 / (1.0 + jnp.exp(-before))
    return before, gate


def pair_gradient(unit, inverse, grad_unit, grad_distance):
    along = jnp.sum(grad_unit * unit, axis=0, keepdims=True)
    return inverse * (grad_unit - unit * along) + unit * grad_distance


def stack_rows(rows):
    where = iota((8, rows[0].shape[1]), 0)
    out = jnp.zeros((8, rows[0].shape[1]), F32)
    for r, row in enumerate(rows):
        out = jnp.where(where == r, row, out)
    return out


def flip(matrix):
    size = matrix.shape[1]
    eye = (iota((size, size), 0) == iota((size, size), 1)).astype(F32).astype(BF16)
    return dot_nt(eye, matrix).astype(BF16)


def weights_kernel(
    embedding, radial_in, radial_out_one, radial_out_two, mix_one, mix_two, readout,
    emb_t, win_t, one_t, two_t, mix_a, mix_b, mix_two_t, spread, read_t, rests,
):
    emb = jnp.concatenate([embedding[...].astype(F32), jnp.zeros((1, C), F32)], axis=0).astype(BF16)
    emb_t[...] = flip(emb)
    for t in range(2):
        win_t[t] = flip(radial_in[t])
        mix_two_t[t] = flip(mix_two[t])
    one_t[...] = flip(radial_out_one[...])
    two_t[...] = flip(radial_out_two[...])
    for k in range(3):
        mix_a[:, k * C : (k + 1) * C] = flip(mix_one[k + 1])
    for k in range(2):
        mix_b[:, k * C : (k + 1) * C] = flip(mix_one[k + 4])
    pe_high, pe_low = split(dot_nt(flip(mix_one[0]), emb))
    spread[...] = jnp.concatenate([pe_high.astype(F32), pe_low.astype(F32)], axis=1).astype(BF16)
    read = jnp.concatenate([readout[...], jnp.zeros((LANES - 2, C), F32)], axis=0)
    read_t[...] = read.T
    read_high, read_low = split(read[0:16])
    for k in range(3):
        rests[k * C : (k + 1) * C, :] = dot_nt(mix_two[k + 2], read_high) + dot_nt(mix_two[k + 2], read_low)


def renamed(index):
    block = (index - SLOTS) >> 4
    nines = (block * 57) >> 9
    threes = (block * 11) >> 5
    turned = (block - threes * 3) * 9 + (threes - nines * 3) * 3 + nines
    return jnp.where(index < SLOTS, index, SLOTS + turned * EXPORT + (index & (EXPORT - 1))).astype(F32)


def pack_kernel(exports, counts, positions, species, neighbours, packed, payload, picked, count):
    even = renamed(neighbours[pl.ds(0, COLUMNS, stride=2), :])
    odd = renamed(neighbours[pl.ds(1, COLUMNS, stride=2), :])
    lane = iota((8, LANES), 1) % EXPORT
    row = iota((EXPORT, LANES), 0)
    source = jnp.zeros((8, LANES), jnp.int32)
    pick = jnp.zeros((EXPORT, LANES), jnp.int32)
    for e in range(EXPORT):
        slot = exports[e]
        source = jnp.where(lane == e, slot, source)
        pick = jnp.where(row == e, slot, pick)
    picked[...] = pick
    count[...] = jnp.full((1, LANES), counts[0], jnp.int32)
    packed[...] = jnp.zeros_like(packed)
    packed[0:COLUMNS, :] = jnp.concatenate([even, odd], axis=1)
    packed[COLUMNS : COLUMNS + 3, 0:SLOTS] = positions[...]
    packed[COLUMNS + 3 : COLUMNS + 4, 0:SLOTS] = species[...].astype(F32)
    packed[COLUMNS + 4 : COLUMNS + 5, :] = source[0:1, :].astype(F32)
    packed[COLUMNS + 5 : COLUMNS + 6, :] = jnp.full((1, LANES), counts[0], jnp.int32).astype(F32)
    whole = packed[COLUMNS : COLUMNS + 8, :]
    whole = jnp.where(iota((8, LANES), 0) < 4, whole, 0.0)
    payload[...] = jnp.take_along_axis(whole, source, axis=1)


def unpack_kernel(arrived, low, high, own, block, picked, index, count):
    whole = arrived[COLUMNS : COLUMNS + 8, :]
    whole = jnp.where(iota((8, LANES), 0) < 4, whole, 0.0)
    own[...] = whole
    exports = arrived[COLUMNS + 4 : COLUMNS + 5, :]
    count[...] = arrived[COLUMNS + 5 : COLUMNS + 6, :].astype(jnp.int32)
    mine = iota((EXPORT, LANES), 1) == iota((EXPORT, LANES), 0)
    pick = jnp.sum(jnp.where(mine, exports, 0.0), axis=1, keepdims=True)
    picked[...] = jnp.broadcast_to(pick, (EXPORT, LANES)).astype(jnp.int32)
    source = jnp.broadcast_to(exports, (8, LANES)).astype(jnp.int32)
    block[0] = low[...]
    block[1] = jnp.take_along_axis(whole, source, axis=1)
    block[2] = high[...]
    for m in range(COLUMNS):
        index[:, m * LANES : (m + 1) * LANES] = arrived[m : m + 1, :].astype(jnp.int32)


def first_kernel(
    count_ref, own, low, mid, high, index, picked, win_t, wout_t, mix_a, mix_b, spread, emb_t, read_t,
    facts_out, basis_out, slope_out, own_rows, outgoing, sums, energy,
):
    count = count_ref[...]
    group = iota((8, LANES), 1) // EXPORT
    rows8 = iota((8, 1), 0)
    tiles = [own[...]] + [jnp.zeros((8, LANES), F32) for _ in range(3)]
    slabs = (low, mid, high)
    for b in range(27):
        oz, oy, ox = b // 9 - 1, b // 3 % 3 - 1, b % 3 - 1
        entry = SLOTS + b * EXPORT
        shift = jnp.where(rows8 == 0, DOMAIN_LENGTH * ox, 0.0)
        shift = jnp.where(rows8 == 1, DOMAIN_LENGTH * oy, shift)
        shift = jnp.where(rows8 == 2, DOMAIN_LENGTH * oz, shift)
        tile = entry // LANES
        at = entry % LANES // EXPORT
        tiles[tile] = jnp.where(group == at, slabs[oz + 1][b % 9] + shift, tiles[tile])
    whole = jnp.concatenate(tiles, axis=1)
    facts, basis, basis_slope = geometry(whole, index[...], count)
    facts_out[...] = facts
    basis_out[...] = basis
    slope_out[...] = basis_slope
    before, gate = hidden_of(win_t[0], basis)
    hidden = (before * gate).astype(BF16)
    species = species_of(facts)
    a0 = jnp.zeros((C, LANES), F32)
    a1 = [jnp.zeros((C, LANES), F32) for _ in range(3)]
    for m in range(COLUMNS):
        radial = dot_nn(wout_t[...], column(hidden, m))
        source = dot_nn(spread[...], column(species, m))
        a0 = a0 + radial[:C] * source
        t = radial[C:] * source
        for x in range(3):
            a1[x] = a1[x] + t * column(facts[x : x + 1], m)
    a0 = fold(a0) * NORM
    a1 = [fold(v) * NORM for v in a1]
    for x, v in enumerate([a0] + a1):
        sums[x * C : (x + 1) * C, :] = v
    quad = a1[0] * a1[0] + a1[1] * a1[1] + a1[2] * a1[2]
    own_kind = (iota((8, LANES), 0) == whole[3:4, :LANES].astype(jnp.int32)).astype(F32).astype(BF16)
    own_kind = jnp.where(iota((8, LANES), 1) < SLOTS, own_kind.astype(F32), 0.0).astype(BF16)
    scalar = dot_nn(emb_t[...], own_kind)
    scalar = scalar + dot_nn(mix_a[...], jnp.concatenate([halves(a0), halves(a0 * a0), halves(quad)], axis=0))
    scalar = fold(scalar)
    top = jnp.concatenate([halves(v) for v in a1], axis=1)
    bottom = jnp.concatenate([halves(a0 * v) for v in a1], axis=1)
    vector = dot_nn(mix_b[...], jnp.concatenate([top, bottom], axis=0))
    parts = [scalar] + [fold(column(vector, x)) for x in range(3)]
    features = jnp.concatenate(parts, axis=0).astype(BF16)
    rounded = features[:C].astype(F32)
    row_energy = jnp.sum(scalar * read_t[:, 0:1] + rounded * read_t[:, 1:2], axis=0, keepdims=True)
    energy[...] = row_energy * live_row(count)
    lanes = iota((SLOTS, LANES), 1)
    eye = (lanes == iota((SLOTS, LANES), 0)).astype(F32).astype(BF16)
    chosen = (iota((EXPORT, LANES), 1) == picked[...]).astype(F32).astype(BF16)
    own_rows[...] = dot_nt(eye, features).astype(BF16)
    outgoing[...] = dot_nt(chosen, features).astype(BF16)


def second_kernel(
    count_ref, facts_ref, basis, slope, own_rows, low, mid, high, index, win_t, win, wout_t, wout, mix_t, rests, read,
    grad_own, grad_low, grad_mid, grad_high, pair_out, energy,
    feats, turned, onehot, radial, source, grad_radial, grad_source,
):
    count = count_ref[...]
    ids = index[...]
    facts = facts_ref[...]
    unit, inverse = unit_of(facts), facts[3:4, :]
    before, gate = hidden_of(win_t[1], basis[...])
    hidden = (before * gate).astype(BF16)
    feats[0:SLOTS, :] = own_rows[...]
    feats[SLOTS : SLOTS + SLAB, :] = low[...]
    feats[SLOTS + SLAB : SLOTS + 2 * SLAB, :] = mid[...]
    feats[SLOTS + 2 * SLAB : SLOTS + 3 * SLAB, :] = high[...]
    feats[SLOTS + 3 * SLAB :, :] = jnp.zeros((TABLE - SLOTS - 3 * SLAB, 4 * C), BF16)
    eye = (iota((C, C), 0) == iota((C, C), 1)).astype(F32).astype(BF16)
    for c in range(4):
        turned[c * C : (c + 1) * C, :] = dot_nt(eye, feats[:, c * C : (c + 1) * C]).astype(BF16)
    entry = iota((TABLE, LANES), 0)
    for m in range(COLUMNS):
        onehot[:, m * LANES : (m + 1) * LANES] = (entry == column(ids, m)).astype(F32).astype(BF16)
    units = [[column(unit[x : x + 1], m) for m in range(COLUMNS)] for x in range(3)]
    wide = 2 * LANES
    a0 = jnp.zeros((C, LANES), F32)
    a1 = [jnp.zeros((C, LANES), F32) for _ in range(3)]
    for w in range(PAIRS // wide):
        at = slice(w * wide, (w + 1) * wide)
        radial[:, at] = dot_nn(wout_t[...], hidden[:, at])
        picked = dot_nn(turned[...], onehot[:, at]).astype(BF16)
        for c in range(4):
            source[c * C : (c + 1) * C, at] = dot_nn(mix_t[min(c, 1)], picked[c * C : (c + 1) * C])
        for m in (2 * w, 2 * w + 1):
            here = slice(m * LANES, (m + 1) * LANES)
            s = source[0:C, here]
            v = [source[(x + 1) * C : (x + 2) * C, here] for x in range(3)]
            u = [units[x][m] for x in range(3)]
            along = v[0] * u[0] + v[1] * u[1] + v[2] * u[2]
            a0 = a0 + radial[0:C, here] * s + radial[3 * C :, here] * along
            t = radial[C : 2 * C, here] * s
            r3 = radial[2 * C : 3 * C, here]
            for x in range(3):
                a1[x] = a1[x] + t * u[x] + r3 * v[x]
    a0 = fold(a0) * NORM
    a1 = [fold(v) * NORM for v in a1]
    quad = a1[0] * a1[0] + a1[1] * a1[1] + a1[2] * a1[2]
    m2, m3, m4 = [rests[k * C : (k + 1) * C, 1:2] for k in range(3)]
    live = live_row(count)
    energy[...] = live * jnp.sum(a0 * m2 + a0 * a0 * m3 + quad * m4, axis=0, keepdims=True)
    live = live * NORM
    d0 = (m2 + 2.0 * a0 * m3) * live
    d1 = [2.0 * v * m4 * live for v in a1]
    grad_units = [[], [], []]
    for m in range(COLUMNS):
        here = slice(m * LANES, (m + 1) * LANES)
        s = source[0:C, here]
        v = [source[(x + 1) * C : (x + 2) * C, here] for x in range(3)]
        u = [units[x][m] for x in range(3)]
        r1, r2, r3, r4 = [radial[k * C : (k + 1) * C, here] for k in range(4)]
        along = v[0] * u[0] + v[1] * u[1] + v[2] * u[2]
        slant = d1[0] * u[0] + d1[1] * u[1] + d1[2] * u[2]
        parts = (d0 * s, s * slant, d1[0] * v[0] + d1[1] * v[1] + d1[2] * v[2], d0 * along)
        for k in range(4):
            high_part, low_part = split(parts[k])
            grad_radial[k * C : (k + 1) * C, here] = high_part
            grad_radial[(k + 4) * C : (k + 5) * C, here] = low_part
        grad_source[0:C, here] = (r1 * d0 + r2 * slant).astype(BF16)
        q = d0 * r4
        t = r2 * s
        for x in range(3):
            grad_source[(x + 1) * C : (x + 2) * C, here] = (q * u[x] + r3 * d1[x]).astype(BF16)
            grad_units[x].append(jnp.sum(q * v[x] + t * d1[x], axis=0, keepdims=True))
    grad_unit = stack_rows([jnp.concatenate(g, axis=1) for g in grad_units])
    grad_distance = grad_distance_of(wout, win[1], grad_radial, before, gate, slope[...])
    pair_out[...] = pair_gradient(unit, inverse, grad_unit, grad_distance)
    grad_projected = dot_nt(onehot[...], grad_source[...])
    outs = (grad_low, grad_mid, grad_high)
    live_rows = (iota((SLOTS, 1), 0) < count[:, 0:1]).astype(F32)
    for c in range(4):
        at = slice(c * C, (c + 1) * C)
        high_part, low_part = split(grad_projected[:, at])
        rows = dot_nn(high_part, mix_t[min(c, 1)]) + dot_nn(low_part, mix_t[min(c, 1)])
        mine = rows[0:SLOTS]
        if c == 0:
            mine = mine + live_rows * read[1:2, :]
        grad_own[:, at] = mine
        for k in range(3):
            begin = SLOTS + k * SLAB
            outs[k][:, at] = rows[begin : begin + SLAB].astype(BF16)


def third_kernel(
    count_ref, facts_ref, basis, slope, sums, grad_own, back, picked, pair_in, index, energy_one, energy_two,
    win_t, win, wout_t, wout, mix_one, spread, read_t,
    grad_mine, grad_low, grad_mid, grad_high,
    onehot, grad_radial,
):
    count = count_ref[...]
    ids = index[...]
    facts = facts_ref[...]
    unit, inverse = unit_of(facts), facts[3:4, :]
    before, gate = hidden_of(win_t[0], basis[...])
    hidden = (before * gate).astype(BF16)
    species = species_of(facts)
    entry = iota((TABLE, LANES), 0)
    for m in range(COLUMNS):
        onehot[:, m * LANES : (m + 1) * LANES] = (entry == column(ids, m)).astype(F32).astype(BF16)
    mine = grad_own[...]
    mine_high = mine.astype(BF16)
    mine_low = (mine - mine_high.astype(F32)).astype(BF16)
    came = back[...].astype(F32)
    came_high = came.astype(BF16)
    came_low = (came - came_high.astype(F32)).astype(BF16)
    eye = (iota((SLOTS, LANES), 1) % SLOTS == iota((SLOTS, LANES), 0)).astype(F32).astype(BF16)
    chosen = (iota((EXPORT, LANES), 1) % SLOTS == picked[...]).astype(F32).astype(BF16)
    left = jnp.concatenate([mine_high, mine_low, came_high, came_low], axis=0)
    right = jnp.concatenate([eye, eye, chosen, chosen], axis=0)
    grads = dot_tn(left, right)
    live = live_row(count)
    gs = grads[0:C] + read_t[:, 0:1] * live
    gv = [grads[(x + 1) * C : (x + 2) * C] for x in range(3)]
    a0 = sums[0:C, :]
    a1 = [sums[(x + 1) * C : (x + 2) * C, :] for x in range(3)]
    scalar_parts = halves(gs)
    vector_parts = jnp.concatenate([halves(g) for g in gv], axis=1)
    first = jnp.concatenate([fold(dot_nn(mix_one[k], scalar_parts)) for k in (1, 2, 3)], axis=0)
    others = jnp.concatenate([fold_columns(dot_nn(mix_one[k], vector_parts)) for k in (4, 5)], axis=0)
    straight = [column(others[0:C], x) for x in range(3)]
    crossed = [column(others[C : 2 * C], x) for x in range(3)]
    scale = live * NORM
    d0 = first[0:C] + 2.0 * a0 * first[C : 2 * C]
    for x in range(3):
        d0 = d0 + a1[x] * crossed[x]
    d0 = d0 * scale
    d1 = [(straight[x] + a0 * crossed[x] + 2.0 * a1[x] * first[2 * C : 3 * C]) * scale for x in range(3)]
    grad_units = [[], [], []]
    for m in range(COLUMNS):
        here = slice(m * LANES, (m + 1) * LANES)
        r2 = dot_nn(wout_t[C : 2 * C, :], column(hidden, m))
        source = dot_nn(spread[...], column(species, m))
        u = [column(unit[x : x + 1], m) for x in range(3)]
        slant = d1[0] * u[0] + d1[1] * u[1] + d1[2] * u[2]
        parts = (d0 * source, slant * source)
        for k in range(2):
            high_part, low_part = split(parts[k])
            grad_radial[k * C : (k + 1) * C, here] = high_part
            grad_radial[(k + 2) * C : (k + 3) * C, here] = low_part
        q = r2 * source
        for x in range(3):
            grad_units[x].append(jnp.sum(q * d1[x], axis=0, keepdims=True))
    grad_unit = stack_rows([jnp.concatenate(g, axis=1) for g in grad_units])
    grad_distance = grad_distance_of(wout, win[0], grad_radial, before, gate, slope[...])
    pairs = pair_in[...] + pair_gradient(unit, inverse, grad_unit, grad_distance)
    pair_high = pairs.astype(BF16)
    pair_low = (pairs - pair_high.astype(F32)).astype(BF16)
    both = jnp.concatenate([pair_high.astype(F32), pair_low.astype(F32)], axis=0).astype(BF16)
    spread_back = dot_nt(both, onehot[...])
    grads = spread_back[0:8] + spread_back[8:16]
    total = column(pairs, 0)
    for m in range(1, COLUMNS):
        total = total + column(pairs, m)
    energies = live * (energy_one[...] + energy_two[...])
    grad_mine[...] = jnp.where(iota((8, LANES), 0) == 3, energies, column(grads, 0) - fold(total))
    outs = (grad_low, grad_mid, grad_high)
    for b in range(27):
        at = SLOTS + b * EXPORT
        tile = column(grads, at // LANES)
        offset = at % LANES
        if offset:
            tile = pltpu.roll(tile, LANES - offset, 1)
        outs[b // 9][b % 9] = tile


def fold_columns(values):
    count = values.shape[1] // LANES
    return jnp.concatenate([fold(column(values, x)) for x in range(count)], axis=1)


def last_kernel(count, main, from_low, from_high, picked, forces, energies):
    same = iota((EXPORT, LANES), 1) == picked[...]
    entry = jnp.sum(jnp.where(same, iota((EXPORT, LANES), 0), 0), axis=0, keepdims=True)
    hit = jnp.sum(same.astype(F32), axis=0, keepdims=True)
    back = main[8:16, :] + from_low[...] + from_high[...]
    came = jnp.take_along_axis(back, jnp.broadcast_to(entry, (8, LANES)), axis=1)
    total = main[0:8, :] + came * hit
    forces[...] = -total[0:3, 0:SLOTS]
    energies[...] = (main[3:4, :] * live_row(count[...]))[:, 0:SLOTS]


def call(kernel, outs, specs, scratch=(), limit=None, smem=0, cost=None):
    in_specs = [pl.BlockSpec(memory_space=pltpu.SMEM)] * smem
    in_specs += [pl.BlockSpec(memory_space=pltpu.VMEM)] * (len(specs) - smem)
    return pl.pallas_call(
        kernel,
        out_shape=[jax.ShapeDtypeStruct(s, t) for s, t in outs],
        in_specs=in_specs,
        out_specs=[pl.BlockSpec(memory_space=pltpu.VMEM)] * len(outs),
        scratch_shapes=[pltpu.VMEM(s, t) for s, t in scratch],
        compiler_params=pltpu.CompilerParams(vmem_limit_bytes=limit or (16 << 20)),
        cost_estimate=cost,
    )(*specs)


DOMAINS = [(x, y, z) for x in range(16) for y in range(4) for z in range(8)]


def given(x, y, z):
    return (x * 4 + y) * 8 + z


def seat(x, y, z):
    x, y, z = x % 16, y % 4, z % 8
    return given(z // 2 * 4 + x // 8 * 2 + z % 2, y, x % 8)


def move_in(step):
    return [(given(x, y, z), seat(x + step, y, z)) for x, y, z in DOMAINS]


def move_out(step):
    return [(seat(x, y, z), given((x + step) % 16, y, z)) for x, y, z in DOMAINS]


def moves(step):
    return [(seat(*d), seat(*(a + b for a, b in zip(d, step)))) for d in DOMAINS]


UP = ((1, 0, 0), (0, 1, 0), (0, 0, 1))
DOWN = ((-1, 0, 0), (0, -1, 0), (0, 0, -1))


def send(value, step):
    return lax.ppermute(value, AXES, moves(step))


def spread_halo(block, first=0):
    for axis in range(first, 2):
        low = send(block, UP[axis])
        high = send(block, DOWN[axis])
        block = jnp.concatenate([low, block, high], axis=0)
    return send(block, UP[2]), block, send(block, DOWN[2])


def gather_halo(low, mid, high, last=0):
    for axis in range(2, last - 1, -1):
        from_low = send(high, UP[axis])
        from_high = send(low, DOWN[axis])
        block = mid + from_low + from_high
        if axis:
            third = block.shape[0] // 3
            low, mid, high = block[:third], block[third : 2 * third], block[2 * third :]
    return block


def body(
    positions, species, counts, neighbours, exports, embedding, radial_in,
    radial_out_one, radial_out_two, mix_one, mix_two, readout,
):
    packed, payload, picked_here, count_here = call(
        pack_kernel,
        [((24, LANES), F32), ((8, LANES), F32), ((EXPORT, LANES), jnp.int32), ((1, LANES), jnp.int32)],
        [exports, counts, positions, species.reshape(1, SLOTS), neighbours],
        smem=2,
    )
    emb_t, win_t, one_t, two_t, mix_a, mix_b, mix_two_t, spread, read_t, rests = call(
        weights_kernel,
        [
            ((C, 8), BF16),
            ((2, RH, NB), BF16),
            ((2 * C, RH), BF16),
            ((4 * C, RH), BF16),
            ((C, 3 * C), BF16),
            ((C, 2 * C), BF16),
            ((2, C, C), BF16),
            ((C, 16), BF16),
            ((C, LANES), F32),
            ((3 * C, 16), F32),
        ],
        [embedding, radial_in, radial_out_one, radial_out_two, mix_one, mix_two, readout],
        cost=pl.CostEstimate(flops=200_000_000, bytes_accessed=2_000_000, transcendentals=0),
    )
    arrived = lax.ppermute(packed, AXES, move_in(0))
    low = lax.ppermute(payload, AXES, move_in(1))
    high = lax.ppermute(payload, AXES, move_in(-1))
    (
        arrived, low, high, emb_t, win_t, one_t, two_t, mix_a, mix_b, mix_two_t, spread, read_t, rests,
        radial_in, radial_out_one, radial_out_two, mix_one, readout,
    ) = lax.optimization_barrier((
        arrived, low, high, emb_t, win_t, one_t, two_t, mix_a, mix_b, mix_two_t, spread, read_t, rests,
        radial_in, radial_out_one, radial_out_two, mix_one, readout,
    ))
    own, block, picked, index, count = call(
        unpack_kernel,
        [
            ((8, LANES), F32),
            ((3, 8, LANES), F32),
            ((EXPORT, LANES), jnp.int32),
            ((1, PAIRS), jnp.int32),
            ((1, LANES), jnp.int32),
        ],
        [arrived, low, high],
    )
    low, mid, high = spread_halo(block, 1)
    facts, basis, slope, own_rows, outgoing, sums, energy_one = call(
        first_kernel,
        [
            ((8, PAIRS), F32),
            ((8, PAIRS), BF16),
            ((8, PAIRS), F32),
            ((SLOTS, 4 * C), BF16),
            ((EXPORT, 4 * C), BF16),
            ((4 * C, LANES), F32),
            ((1, LANES), F32),
        ],
        [count, own, low, mid, high, index, picked, win_t, one_t, mix_a, mix_b, spread, emb_t, read_t],
    )
    low, mid, high = spread_halo(outgoing)
    grad_own, grad_low, grad_mid, grad_high, pairs, energy_two = call(
        second_kernel,
        [
            ((SLOTS, 4 * C), F32),
            ((SLAB, 4 * C), BF16),
            ((SLAB, 4 * C), BF16),
            ((SLAB, 4 * C), BF16),
            ((8, PAIRS), F32),
            ((1, LANES), F32),
        ],
        [
            count, facts, basis, slope, own_rows, low, mid, high, index, win_t, radial_in, two_t,
            radial_out_two, mix_two_t, rests, readout,
        ],
        scratch=[
            ((TABLE, 4 * C), BF16),
            ((4 * C, TABLE), BF16),
            ((TABLE, PAIRS), BF16),
            ((4 * C, PAIRS), F32),
            ((4 * C, PAIRS), F32),
            ((8 * C, PAIRS), BF16),
            ((4 * C, PAIRS), BF16),
        ],
        limit=48 << 20,
    )
    back = gather_halo(grad_low, grad_mid, grad_high)
    grad_mine, grad_low, grad_mid, grad_high = call(
        third_kernel,
        [((8, LANES), F32), ((9, 8, LANES), F32), ((9, 8, LANES), F32), ((9, 8, LANES), F32)],
        [
            count, facts, basis, slope, sums, grad_own, back, picked, pairs, index, energy_one, energy_two,
            win_t, radial_in, one_t, radial_out_one, mix_one, spread, read_t,
        ],
        scratch=[((TABLE, PAIRS), BF16), ((4 * C, PAIRS), BF16)],
        limit=32 << 20,
    )
    block = gather_halo(grad_low, grad_mid, grad_high, 1)
    main = lax.ppermute(jnp.concatenate([grad_mine, block[1]], axis=0), AXES, move_out(0))
    from_low = lax.ppermute(block[2], AXES, move_out(1))
    from_high = lax.ppermute(block[0], AXES, move_out(-1))
    forces, energies = call(
        last_kernel,
        [((3, SLOTS), F32), ((1, SLOTS), F32)],
        [count_here, main, from_low, from_high, picked_here],
    )
    return forces, energies.reshape(SLOTS)


def solution(mesh):
    whole = P()
    split = P(AXES)
    in_specs = (P(None, AXES), split, split, P(None, AXES), split) + (whole,) * 7
    out_specs = (P(None, AXES), split)
    return jax.shard_map(body, mesh=mesh, in_specs=in_specs, out_specs=out_specs, check_vma=False)
```

```python
import math

import jax
import jax.numpy as jnp
from jax import lax
from jax.experimental import pallas as pl
from jax.experimental.pallas import tpu as pltpu
from jax.sharding import PartitionSpec as P

C = 128
NB = 8
RH = 64
NSPEC = 7
SLOTS = 64
DEPTH = 32
EXPORT = 16
PAIRS = SLOTS * DEPTH
SLAB = 9 * EXPORT
TABLE = 512
LANES = 128
COLUMNS = PAIRS // LANES
DOMAIN_LENGTH = 6.0
CUTOFF = 6.0
SOFTEN = 0.25
NORM = 1.0 / math.sqrt(DEPTH)
AXES = ("gx", "gy", "gz")
F32 = jnp.float32
BF16 = jnp.bfloat16


def dot_nn(a, b):
    return lax.dot_general(a, b, (((1,), (0,)), ((), ())), preferred_element_type=F32)


def dot_nt(a, b):
    return lax.dot_general(a, b, (((1,), (1,)), ((), ())), preferred_element_type=F32)


def dot_tn(a, b):
    return lax.dot_general(a, b, (((0,), (0,)), ((), ())), preferred_element_type=F32)


def iota(shape, dim):
    return lax.broadcasted_iota(jnp.int32, shape, dim)


def column(values, m):
    return values[:, m * LANES : (m + 1) * LANES]


def halves(values):
    high = values.astype(BF16)
    low = (values - high.astype(F32)).astype(BF16)
    return jnp.where(iota(values.shape, 1) % LANES < SLOTS, high.astype(F32), low.astype(F32)).astype(BF16)


def fold(values):
    return values + pltpu.roll(values, SLOTS, 1)


def live_row(count):
    return (iota((1, LANES), 1) % SLOTS < count).astype(F32)


def gather_entries(table, index):
    parts = []
    for m in range(COLUMNS):
        ids = jnp.broadcast_to(column(index, m), (8, LANES))
        low = ids & (LANES - 1)
        high = ids >> 7
        found = jnp.take_along_axis(column(table, 0), low, axis=1)
        for v in range(1, TABLE // LANES):
            found = jnp.where(high == v, jnp.take_along_axis(column(table, v), low, axis=1), found)
        parts.append(found)
    return jnp.concatenate(parts, axis=1)


def sincos_pi(turns):
    whole = jnp.floor(turns + 0.5)
    part = turns - whole
    sign = 1.0 - 2.0 * (whole - 2.0 * jnp.floor(whole * 0.5))
    square = part * part
    sine = 0.0
    cosine = 0.0
    for n in range(6, -1, -1):
        cosine = cosine * square + (-1.0) ** n * math.pi ** (2 * n) / math.factorial(2 * n)
    for n in range(5, -1, -1):
        sine = sine * square + (-1.0) ** n * math.pi ** (2 * n + 1) / math.factorial(2 * n + 1)
    return sine * part * sign, cosine * sign


def geometry(table, index, count):
    found = gather_entries(table, index)
    first = column(table, 0)
    centre = jnp.where(iota((8, LANES), 1) < SLOTS, first, pltpu.roll(first, SLOTS, 1))
    centre = jnp.concatenate([centre] * COLUMNS, axis=1)
    rows = iota((8, PAIRS), 0)
    delta = jnp.where(rows < 3, found - centre, 0.0)
    square = jnp.sum(delta * delta, axis=0, keepdims=True) + SOFTEN
    inverse = lax.rsqrt(square)
    distance = square * inverse
    slot = iota((1, PAIRS), 1) % SLOTS
    paired = jnp.where(index != slot, jnp.concatenate([live_row(count)] * COLUMNS, axis=1), 0.0)
    scaled = jnp.minimum(distance * (1.0 / CUTOFF), 1.0)
    power = scaled * scaled * scaled
    power = power * power
    envelope = 1.0 + power * (-28.0 + scaled * (48.0 - 21.0 * scaled))
    orders = (iota((8, 1), 0) + 1).astype(F32)
    sine, cosine = sincos_pi(orders * scaled)
    weight = envelope * paired * inverse
    basis = (sine * weight).astype(BF16)
    rest = 1.0 - scaled
    slope = (-168.0 / CUTOFF) * (power * rest * rest) / jnp.maximum(scaled, 1e-3)
    basis_slope = weight * cosine * (orders * (math.pi / CUTOFF)) + sine * (
        slope * paired * inverse - weight * inverse
    )
    facts = jnp.where(rows == 3, inverse, jnp.where(rows == 4, found[3:4, :], delta * inverse))
    return facts, basis, basis_slope


def unit_of(facts):
    return jnp.where(iota((8, PAIRS), 0) < 3, facts, 0.0)


def species_of(facts):
    return (iota((16, PAIRS), 0) % 8 == facts[4:5, :].astype(jnp.int32)).astype(F32).astype(BF16)


def split(values):
    high = values.astype(BF16)
    return high, (values - high.astype(F32)).astype(BF16)


def keep(values):
    return values.astype(BF16).astype(F32)


def grad_distance_of(wout, win, grad_radial, before, gate, basis_slope):
    half = grad_radial.shape[0] // 2
    grad_hidden = keep(dot_nn(wout[...], grad_radial[0:half, :]) + dot_nn(wout[...], grad_radial[half:, :]))
    high, low = split(grad_hidden * (gate * (1.0 + before * (1.0 - gate))))
    grad_basis = keep(dot_nn(win, high) + dot_nn(win, low))
    return jnp.sum(grad_basis * basis_slope, axis=0, keepdims=True)


def hidden_of(weights, basis):
    before = dot_nn(weights, basis)
    gate = 1.0 / (1.0 + jnp.exp(-before))
    return before, gate


def pair_gradient(unit, inverse, grad_unit, grad_distance):
    along = jnp.sum(grad_unit * unit, axis=0, keepdims=True)
    return inverse * (grad_unit - unit * along) + unit * grad_distance


def stack_rows(rows):
    where = iota((8, rows[0].shape[1]), 0)
    out = jnp.zeros((8, rows[0].shape[1]), F32)
    for r, row in enumerate(rows):
        out = jnp.where(where == r, row, out)
    return out


def flip(matrix):
    size = matrix.shape[1]
    eye = (iota((size, size), 0) == iota((size, size), 1)).astype(F32).astype(BF16)
    return dot_nt(eye, matrix).astype(BF16)


def fetch(pairs, semaphores):
    copies = [pltpu.make_async_copy(there, here, semaphores.at[k]) for k, (there, here) in enumerate(pairs)]
    for copy in copies:
        copy.start()
    for copy in copies:
        copy.wait()


def weights_kernel(
    embedding_far, radial_in_far, radial_out_one_far, radial_out_two_far, mix_one_far, mix_two_far, readout_far,
    radial_in, radial_out_one, radial_out_two, mix_one, readout,
    emb_t, win_t, one_t, two_t, mix_a, mix_b, mix_two_t, spread, read_t, rests,
    embedding, mix_two, semaphores,
):
    fetch(
        (
            (mix_one_far, mix_one),
            (mix_two_far, mix_two),
            (radial_out_two_far, radial_out_two),
            (radial_out_one_far, radial_out_one),
            (radial_in_far, radial_in),
            (embedding_far, embedding),
            (readout_far, readout),
        ),
        semaphores,
    )
    emb = jnp.concatenate([embedding[...].astype(F32), jnp.zeros((1, C), F32)], axis=0).astype(BF16)
    emb_t[...] = flip(emb)
    for t in range(2):
        win_t[t] = flip(radial_in[t])
        mix_two_t[t] = flip(mix_two[t])
    one_t[...] = flip(radial_out_one[...])
    two_t[...] = flip(radial_out_two[...])
    for k in range(3):
        mix_a[:, k * C : (k + 1) * C] = flip(mix_one[k + 1])
    for k in range(2):
        mix_b[:, k * C : (k + 1) * C] = flip(mix_one[k + 4])
    pe_high, pe_low = split(dot_nt(flip(mix_one[0]), emb))
    spread[...] = jnp.concatenate([pe_high.astype(F32), pe_low.astype(F32)], axis=1).astype(BF16)
    read = jnp.concatenate([readout[...], jnp.zeros((LANES - 2, C), F32)], axis=0)
    read_t[...] = read.T
    read_high, read_low = split(read[0:16])
    for k in range(3):
        rests[k * C : (k + 1) * C, :] = dot_nt(mix_two[k + 2], read_high) + dot_nt(mix_two[k + 2], read_low)


def renamed(index):
    block = (index - SLOTS) >> 4
    nines = (block * 57) >> 9
    threes = (block * 11) >> 5
    turned = (block - threes * 3) * 9 + (threes - nines * 3) * 3 + nines
    return jnp.where(index < SLOTS, index, SLOTS + turned * EXPORT + (index & (EXPORT - 1))).astype(F32)


def pack_kernel(
    counts, exports_far, positions_far, species_far, neighbours_far, packed,
    exports, positions, species, neighbours, semaphores,
):
    fetch(
        (
            (neighbours_far, neighbours),
            (positions_far, positions),
            (species_far, species),
            (exports_far, exports),
        ),
        semaphores,
    )
    even = renamed(neighbours[pl.ds(0, COLUMNS, stride=2), :])
    odd = renamed(neighbours[pl.ds(1, COLUMNS, stride=2), :])
    lane = iota((1, LANES), 1) % EXPORT
    source = jnp.zeros((1, LANES), jnp.int32)
    for e in range(EXPORT):
        source = jnp.where(lane == e, exports[e], source)
    packed[...] = jnp.zeros_like(packed)
    packed[0:COLUMNS, :] = jnp.concatenate([even, odd], axis=1)
    packed[COLUMNS : COLUMNS + 3, 0:SLOTS] = positions[...]
    packed[COLUMNS + 3 : COLUMNS + 4, 0:SLOTS] = species[...].astype(F32)
    packed[COLUMNS + 4 : COLUMNS + 5, :] = source.astype(F32)
    packed[COLUMNS + 5 : COLUMNS + 6, :] = jnp.full((1, LANES), counts[0], jnp.int32).astype(F32)


def unpack_kernel(arrived, own, payload, picked, index, count):
    whole = arrived[COLUMNS : COLUMNS + 8, :]
    whole = jnp.where(iota((8, LANES), 0) < 4, whole, 0.0)
    own[...] = whole
    exports = arrived[COLUMNS + 4 : COLUMNS + 5, :]
    count[...] = arrived[COLUMNS + 5 : COLUMNS + 6, :].astype(jnp.int32)
    mine = iota((EXPORT, LANES), 1) == iota((EXPORT, LANES), 0)
    pick = jnp.sum(jnp.where(mine, exports, 0.0), axis=1, keepdims=True)
    picked[...] = jnp.broadcast_to(pick, (EXPORT, LANES)).astype(jnp.int32)
    source = jnp.broadcast_to(exports, (8, LANES)).astype(jnp.int32)
    payload[0] = jnp.take_along_axis(whole, source, axis=1)
    for m in range(COLUMNS):
        index[:, m * LANES : (m + 1) * LANES] = arrived[m : m + 1, :].astype(jnp.int32)


def side_kernel(
    facts_ref, basis, index, win_t, one_t, spread,
    onehot, before_one, gate_one, before_two, gate_two, source, slanted,
):
    ids = index[...]
    entry = iota((TABLE, LANES), 0)
    for m in range(COLUMNS):
        onehot[:, m * LANES : (m + 1) * LANES] = (entry == column(ids, m)).astype(F32).astype(BF16)
    before, gate = hidden_of(win_t[1], basis[...])
    before_two[...] = before
    gate_two[...] = gate
    before, gate = hidden_of(win_t[0], basis[...])
    before_one[...] = before
    gate_one[...] = gate
    hidden = (before * gate).astype(BF16)
    species = species_of(facts_ref[...])
    for m in range(COLUMNS):
        here = slice(m * LANES, (m + 1) * LANES)
        found = dot_nn(spread[...], column(species, m))
        source[:, here] = found
        slanted[:, here] = found * dot_nn(one_t[C : 2 * C, :], column(hidden, m))


def first_kernel(
    count_ref, own, low, mid, high, index, picked, win_t, wout_t, mix_a, mix_b, spread, emb_t, read_t,
    facts_out, basis_out, slope_out, own_rows, outgoing, sums, energy,
):
    count = count_ref[...]
    group = iota((8, LANES), 1) // EXPORT
    rows8 = iota((8, 1), 0)
    tiles = [own[...]] + [jnp.zeros((8, LANES), F32) for _ in range(3)]
    slabs = (low, mid, high)
    for b in range(27):
        oz, oy, ox = b // 9 - 1, b // 3 % 3 - 1, b % 3 - 1
        entry = SLOTS + b * EXPORT
        shift = jnp.where(rows8 == 0, DOMAIN_LENGTH * ox, 0.0)
        shift = jnp.where(rows8 == 1, DOMAIN_LENGTH * oy, shift)
        shift = jnp.where(rows8 == 2, DOMAIN_LENGTH * oz, shift)
        tile = entry // LANES
        at = entry % LANES // EXPORT
        tiles[tile] = jnp.where(group == at, slabs[oz + 1][b % 9] + shift, tiles[tile])
    whole = jnp.concatenate(tiles, axis=1)
    facts, basis, basis_slope = geometry(whole, index[...], count)
    facts_out[...] = facts
    basis_out[...] = basis
    slope_out[...] = basis_slope
    before, gate = hidden_of(win_t[0], basis)
    hidden = (before * gate).astype(BF16)
    species = species_of(facts)
    a0 = jnp.zeros((C, LANES), F32)
    a1 = [jnp.zeros((C, LANES), F32) for _ in range(3)]
    for m in range(COLUMNS):
        radial = dot_nn(wout_t[...], column(hidden, m))
        source = dot_nn(spread[...], column(species, m))
        a0 = a0 + radial[:C] * source
        t = radial[C:] * source
        for x in range(3):
            a1[x] = a1[x] + t * column(facts[x : x + 1], m)
    a0 = fold(a0) * NORM
    a1 = [fold(v) * NORM for v in a1]
    for x, v in enumerate([a0] + a1):
        sums[x * C : (x + 1) * C, :] = v
    quad = a1[0] * a1[0] + a1[1] * a1[1] + a1[2] * a1[2]
    own_kind = (iota((8, LANES), 0) == whole[3:4, :LANES].astype(jnp.int32)).astype(F32).astype(BF16)
    own_kind = jnp.where(iota((8, LANES), 1) < SLOTS, own_kind.astype(F32), 0.0).astype(BF16)
    scalar = dot_nn(emb_t[...], own_kind)
    scalar = scalar + dot_nn(mix_a[...], jnp.concatenate([halves(a0), halves(a0 * a0), halves(quad)], axis=0))
    scalar = fold(scalar)
    top = jnp.concatenate([halves(v) for v in a1], axis=1)
    bottom = jnp.concatenate([halves(a0 * v) for v in a1], axis=1)
    vector = dot_nn(mix_b[...], jnp.concatenate([top, bottom], axis=0))
    parts = [scalar] + [fold(column(vector, x)) for x in range(3)]
    features = jnp.concatenate(parts, axis=0).astype(BF16)
    rounded = features[:C].astype(F32)
    row_energy = jnp.sum(scalar * read_t[:, 0:1] + rounded * read_t[:, 1:2], axis=0, keepdims=True)
    energy[...] = row_energy * live_row(count)
    lanes = iota((SLOTS, LANES), 1)
    eye = (lanes == iota((SLOTS, LANES), 0)).astype(F32).astype(BF16)
    chosen = (iota((EXPORT, LANES), 1) == picked[...]).astype(F32).astype(BF16)
    own_rows[...] = dot_nt(eye, features).astype(BF16)
    outgoing[...] = dot_nt(chosen, features).astype(BF16)


def second_kernel(
    count_ref, facts_ref, slope, onehot, before_two, gate_two, own_rows, low, mid, high,
    win, wout_t, wout, mix_t, rests, read,
    grad_own, grad_low, grad_mid, grad_high, pair_out, energy,
    feats, turned, radial, source, grad_radial, grad_source,
):
    count = count_ref[...]
    facts = facts_ref[...]
    unit, inverse = unit_of(facts), facts[3:4, :]
    before, gate = before_two[...], gate_two[...]
    hidden = (before * gate).astype(BF16)
    feats[0:SLOTS, :] = own_rows[...]
    feats[SLOTS : SLOTS + SLAB, :] = low[...]
    feats[SLOTS + SLAB : SLOTS + 2 * SLAB, :] = mid[...]
    feats[SLOTS + 2 * SLAB : SLOTS + 3 * SLAB, :] = high[...]
    feats[SLOTS + 3 * SLAB :, :] = jnp.zeros((TABLE - SLOTS - 3 * SLAB, 4 * C), BF16)
    eye = (iota((C, C), 0) == iota((C, C), 1)).astype(F32).astype(BF16)
    for c in range(4):
        turned[c * C : (c + 1) * C, :] = dot_nt(eye, feats[:, c * C : (c + 1) * C]).astype(BF16)
    units = [[column(unit[x : x + 1], m) for m in range(COLUMNS)] for x in range(3)]
    wide = 2 * LANES
    a0 = jnp.zeros((C, LANES), F32)
    a1 = [jnp.zeros((C, LANES), F32) for _ in range(3)]
    for w in range(PAIRS // wide):
        at = slice(w * wide, (w + 1) * wide)
        radial[:, at] = dot_nn(wout_t[...], hidden[:, at])
        picked = dot_nn(turned[...], onehot[:, at]).astype(BF16)
        for c in range(4):
            source[c * C : (c + 1) * C, at] = dot_nn(mix_t[min(c, 1)], picked[c * C : (c + 1) * C])
        for m in (2 * w, 2 * w + 1):
            here = slice(m * LANES, (m + 1) * LANES)
            s = source[0:C, here]
            v = [source[(x + 1) * C : (x + 2) * C, here] for x in range(3)]
            u = [units[x][m] for x in range(3)]
            along = v[0] * u[0] + v[1] * u[1] + v[2] * u[2]
            a0 = a0 + radial[0:C, here] * s + radial[3 * C :, here] * along
            t = radial[C : 2 * C, here] * s
            r3 = radial[2 * C : 3 * C, here]
            for x in range(3):
                a1[x] = a1[x] + t * u[x] + r3 * v[x]
    a0 = fold(a0) * NORM
    a1 = [fold(v) * NORM for v in a1]
    quad = a1[0] * a1[0] + a1[1] * a1[1] + a1[2] * a1[2]
    m2, m3, m4 = [rests[k * C : (k + 1) * C, 1:2] for k in range(3)]
    live = live_row(count)
    energy[...] = live * jnp.sum(a0 * m2 + a0 * a0 * m3 + quad * m4, axis=0, keepdims=True)
    live = live * NORM
    d0 = (m2 + 2.0 * a0 * m3) * live
    d1 = [2.0 * v * m4 * live for v in a1]
    grad_units = [[], [], []]
    for m in range(COLUMNS):
        here = slice(m * LANES, (m + 1) * LANES)
        s = source[0:C, here]
        v = [source[(x + 1) * C : (x + 2) * C, here] for x in range(3)]
        u = [units[x][m] for x in range(3)]
        r1, r2, r3, r4 = [radial[k * C : (k + 1) * C, here] for k in range(4)]
        along = v[0] * u[0] + v[1] * u[1] + v[2] * u[2]
        slant = d1[0] * u[0] + d1[1] * u[1] + d1[2] * u[2]
        parts = (d0 * s, s * slant, d1[0] * v[0] + d1[1] * v[1] + d1[2] * v[2], d0 * along)
        for k in range(4):
            high_part, low_part = split(parts[k])
            grad_radial[k * C : (k + 1) * C, here] = high_part
            grad_radial[(k + 4) * C : (k + 5) * C, here] = low_part
        grad_source[0:C, here] = (r1 * d0 + r2 * slant).astype(BF16)
        q = d0 * r4
        t = r2 * s
        for x in range(3):
            grad_source[(x + 1) * C : (x + 2) * C, here] = (q * u[x] + r3 * d1[x]).astype(BF16)
            grad_units[x].append(jnp.sum(q * v[x] + t * d1[x], axis=0, keepdims=True))
    grad_unit = stack_rows([jnp.concatenate(g, axis=1) for g in grad_units])
    grad_distance = grad_distance_of(wout, win[1], grad_radial, before, gate, slope[...])
    pair_out[...] = pair_gradient(unit, inverse, grad_unit, grad_distance)
    grad_projected = dot_nt(onehot[...], grad_source[...])
    outs = (grad_low, grad_mid, grad_high)
    live_rows = (iota((SLOTS, 1), 0) < count[:, 0:1]).astype(F32)
    for c in range(4):
        at = slice(c * C, (c + 1) * C)
        high_part, low_part = split(grad_projected[:, at])
        rows = dot_nn(high_part, mix_t[min(c, 1)]) + dot_nn(low_part, mix_t[min(c, 1)])
        mine = rows[0:SLOTS]
        if c == 0:
            mine = mine + live_rows * read[1:2, :]
        grad_own[:, at] = mine
        for k in range(3):
            begin = SLOTS + k * SLAB
            outs[k][:, at] = rows[begin : begin + SLAB].astype(BF16)


def third_kernel(
    count_ref, facts_ref, slope, onehot, before_one, gate_one, sources, slanted, sums, grad_own, back, picked,
    pair_in, energy_one, energy_two, win, wout, mix_one, read_t,
    grad_mine, grad_low, grad_mid, grad_high,
    grad_radial,
):
    count = count_ref[...]
    facts = facts_ref[...]
    unit, inverse = unit_of(facts), facts[3:4, :]
    before, gate = before_one[...], gate_one[...]
    mine = grad_own[...]
    mine_high = mine.astype(BF16)
    mine_low = (mine - mine_high.astype(F32)).astype(BF16)
    came = back[...].astype(F32)
    came_high = came.astype(BF16)
    came_low = (came - came_high.astype(F32)).astype(BF16)
    eye = (iota((SLOTS, LANES), 1) % SLOTS == iota((SLOTS, LANES), 0)).astype(F32).astype(BF16)
    chosen = (iota((EXPORT, LANES), 1) % SLOTS == picked[...]).astype(F32).astype(BF16)
    left = jnp.concatenate([mine_high, mine_low, came_high, came_low], axis=0)
    right = jnp.concatenate([eye, eye, chosen, chosen], axis=0)
    grads = dot_tn(left, right)
    live = live_row(count)
    gs = grads[0:C] + read_t[:, 0:1] * live
    gv = [grads[(x + 1) * C : (x + 2) * C] for x in range(3)]
    a0 = sums[0:C, :]
    a1 = [sums[(x + 1) * C : (x + 2) * C, :] for x in range(3)]
    scalar_parts = halves(gs)
    vector_parts = jnp.concatenate([halves(g) for g in gv], axis=1)
    first = jnp.concatenate([fold(dot_nn(mix_one[k], scalar_parts)) for k in (1, 2, 3)], axis=0)
    others = jnp.concatenate([fold_columns(dot_nn(mix_one[k], vector_parts)) for k in (4, 5)], axis=0)
    straight = [column(others[0:C], x) for x in range(3)]
    crossed = [column(others[C : 2 * C], x) for x in range(3)]
    scale = live * NORM
    d0 = first[0:C] + 2.0 * a0 * first[C : 2 * C]
    for x in range(3):
        d0 = d0 + a1[x] * crossed[x]
    d0 = d0 * scale
    d1 = [(straight[x] + a0 * crossed[x] + 2.0 * a1[x] * first[2 * C : 3 * C]) * scale for x in range(3)]
    grad_units = [[], [], []]
    for m in range(COLUMNS):
        here = slice(m * LANES, (m + 1) * LANES)
        source = sources[:, here]
        u = [column(unit[x : x + 1], m) for x in range(3)]
        slant = d1[0] * u[0] + d1[1] * u[1] + d1[2] * u[2]
        parts = (d0 * source, slant * source)
        for k in range(2):
            high_part, low_part = split(parts[k])
            grad_radial[k * C : (k + 1) * C, here] = high_part
            grad_radial[(k + 2) * C : (k + 3) * C, here] = low_part
        q = slanted[:, here]
        for x in range(3):
            grad_units[x].append(jnp.sum(q * d1[x], axis=0, keepdims=True))
    grad_unit = stack_rows([jnp.concatenate(g, axis=1) for g in grad_units])
    grad_distance = grad_distance_of(wout, win[0], grad_radial, before, gate, slope[...])
    pairs = pair_in[...] + pair_gradient(unit, inverse, grad_unit, grad_distance)
    pair_high = pairs.astype(BF16)
    pair_low = (pairs - pair_high.astype(F32)).astype(BF16)
    both = jnp.concatenate([pair_high.astype(F32), pair_low.astype(F32)], axis=0).astype(BF16)
    spread_back = dot_nt(both, onehot[...])
    grads = spread_back[0:8] + spread_back[8:16]
    total = column(pairs, 0)
    for m in range(1, COLUMNS):
        total = total + column(pairs, m)
    energies = live * (energy_one[...] + energy_two[...])
    grad_mine[...] = jnp.where(iota((8, LANES), 0) == 3, energies, column(grads, 0) - fold(total))
    outs = (grad_low, grad_mid, grad_high)
    for b in range(27):
        at = SLOTS + b * EXPORT
        tile = column(grads, at // LANES)
        offset = at % LANES
        if offset:
            tile = pltpu.roll(tile, LANES - offset, 1)
        outs[b // 9][b % 9] = tile


def fold_columns(values):
    count = values.shape[1] // LANES
    return jnp.concatenate([fold(column(values, x)) for x in range(count)], axis=1)


def last_kernel(grad_mine, back, picked, out):
    same = iota((EXPORT, LANES), 1) == picked[...]
    entry = jnp.sum(jnp.where(same, iota((EXPORT, LANES), 0), 0), axis=0, keepdims=True)
    hit = jnp.sum(same.astype(F32), axis=0, keepdims=True)
    came = jnp.take_along_axis(back[...], jnp.broadcast_to(entry, (8, LANES)), axis=1)
    mine = grad_mine[...]
    out[...] = jnp.where(iota((8, LANES), 0) == 3, mine, -(mine + came * hit))


def finish_kernel(out, forces, energies):
    forces[...] = out[0:3, 0:SLOTS]
    energies[...] = out[3:4, 0:SLOTS]


def call(kernel, outs, specs, scratch=(), limit=None, far=False, cost=None):
    spaces = [pltpu.HBM if far else pltpu.VMEM] * len(specs)
    if far:
        spaces = [space if v.size > 1 else pltpu.SMEM for space, v in zip(spaces, specs)]
        specs = [pltpu.with_memory_space_constraint(v, pltpu.HBM) if v.size > 1 else v for v in specs]
    return pl.pallas_call(
        kernel,
        out_shape=[jax.ShapeDtypeStruct(s, t) for s, t in outs],
        in_specs=[pl.BlockSpec(memory_space=space) for space in spaces],
        out_specs=[pl.BlockSpec(memory_space=pltpu.VMEM)] * len(outs),
        scratch_shapes=[s if not isinstance(s, tuple) else pltpu.VMEM(*s) for s in scratch],
        compiler_params=pltpu.CompilerParams(vmem_limit_bytes=limit or (16 << 20)),
        cost_estimate=cost,
    )(*specs)


DOMAINS = [(x, y, z) for x in range(16) for y in range(4) for z in range(8)]


def given(x, y, z):
    return (x * 4 + y) * 8 + z


def seat(x, y, z):
    x, y, z = (1 - x) % 16, y % 4, (z + 5) % 8
    return given(z // 2 * 4 + x // 8 * 2 + z % 2, y, x % 8)


MOVE_IN = [(given(*d), seat(*d)) for d in DOMAINS]
MOVE_OUT = [(there, here) for here, there in MOVE_IN]


def moves(step):
    return [(seat(*d), seat(*(a + b for a, b in zip(d, step)))) for d in DOMAINS]


UP = ((1, 0, 0), (0, 1, 0), (0, 0, 1))
DOWN = ((-1, 0, 0), (0, -1, 0), (0, 0, -1))


def send(value, step):
    return lax.ppermute(value, AXES, moves(step))


def spread_halo(block):
    for axis in range(2):
        low = send(block, UP[axis])
        high = send(block, DOWN[axis])
        block = jnp.concatenate([low, block, high], axis=0)
    return send(block, UP[2]), block, send(block, DOWN[2])


def gather_halo(low, mid, high):
    for axis in (2, 1, 0):
        from_low = send(high, UP[axis])
        from_high = send(low, DOWN[axis])
        block = mid + from_low + from_high
        if axis:
            third = block.shape[0] // 3
            low, mid, high = block[:third], block[third : 2 * third], block[2 * third :]
    return block


def body(
    positions, species, counts, neighbours, exports, embedding, radial_in,
    radial_out_one, radial_out_two, mix_one, mix_two, readout,
):
    (packed,) = call(
        pack_kernel,
        [((24, LANES), F32)],
        [counts, exports, positions, species.reshape(1, SLOTS), neighbours],
        scratch=[
            pltpu.SMEM((EXPORT,), jnp.int32),
            ((3, SLOTS), F32),
            ((1, SLOTS), jnp.int32),
            ((DEPTH, SLOTS), jnp.int32),
            pltpu.SemaphoreType.DMA((4,)),
        ],
        far=True,
    )
    weights = call(
        weights_kernel,
        [
            ((2, NB, RH), BF16),
            ((RH, 2 * C), BF16),
            ((RH, 4 * C), BF16),
            ((6, C, C), BF16),
            ((2, C), F32),
            ((C, 8), BF16),
            ((2, RH, NB), BF16),
            ((2 * C, RH), BF16),
            ((4 * C, RH), BF16),
            ((C, 3 * C), BF16),
            ((C, 2 * C), BF16),
            ((2, C, C), BF16),
            ((C, 16), BF16),
            ((C, LANES), F32),
            ((3 * C, 16), F32),
        ],
        [embedding, radial_in, radial_out_one, radial_out_two, mix_one, mix_two, readout],
        scratch=[((NSPEC, C), BF16), ((5, C, C), BF16), pltpu.SemaphoreType.DMA((7,))],
        far=True,
        cost=pl.CostEstimate(flops=200_000_000, bytes_accessed=2_000_000, transcendentals=0),
    )
    arrived = lax.ppermute(packed, AXES, MOVE_IN)
    arrived, *weights = lax.optimization_barrier((arrived, *weights))
    (
        radial_in, radial_out_one, radial_out_two, mix_one, readout,
        emb_t, win_t, one_t, two_t, mix_a, mix_b, mix_two_t, spread, read_t, rests,
    ) = weights
    own, payload, picked, index, count = call(
        unpack_kernel,
        [
            ((8, LANES), F32),
            ((1, 8, LANES), F32),
            ((EXPORT, LANES), jnp.int32),
            ((1, PAIRS), jnp.int32),
            ((1, LANES), jnp.int32),
        ],
        [arrived],
    )
    low, mid, high = spread_halo(payload)
    facts, basis, slope, own_rows, outgoing, sums, energy_one = call(
        first_kernel,
        [
            ((8, PAIRS), F32),
            ((8, PAIRS), BF16),
            ((8, PAIRS), F32),
            ((SLOTS, 4 * C), BF16),
            ((EXPORT, 4 * C), BF16),
            ((4 * C, LANES), F32),
            ((1, LANES), F32),
        ],
        [count, own, low, mid, high, index, picked, win_t, one_t, mix_a, mix_b, spread, emb_t, read_t],
    )
    onehot, before_one, gate_one, before_two, gate_two, source, slanted = call(
        side_kernel,
        [
            ((TABLE, PAIRS), BF16),
            ((RH, PAIRS), F32),
            ((RH, PAIRS), F32),
            ((RH, PAIRS), F32),
            ((RH, PAIRS), F32),
            ((C, PAIRS), F32),
            ((C, PAIRS), F32),
        ],
        [facts, basis, index, win_t, one_t, spread],
        cost=pl.CostEstimate(flops=500_000_000, bytes_accessed=6_000_000, transcendentals=0),
    )
    low, mid, high = spread_halo(outgoing)
    grad_own, grad_low, grad_mid, grad_high, pairs, energy_two = call(
        second_kernel,
        [
            ((SLOTS, 4 * C), F32),
            ((SLAB, 4 * C), BF16),
            ((SLAB, 4 * C), BF16),
            ((SLAB, 4 * C), BF16),
            ((8, PAIRS), F32),
            ((1, LANES), F32),
        ],
        [
            count, facts, slope, onehot, before_two, gate_two, own_rows, low, mid, high, radial_in, two_t,
            radial_out_two, mix_two_t, rests, readout,
        ],
        scratch=[
            ((TABLE, 4 * C), BF16),
            ((4 * C, TABLE), BF16),
            ((4 * C, PAIRS), F32),
            ((4 * C, PAIRS), F32),
            ((8 * C, PAIRS), BF16),
            ((4 * C, PAIRS), BF16),
        ],
        limit=36 << 20,
    )
    back = gather_halo(grad_low, grad_mid, grad_high)
    grad_mine, grad_low, grad_mid, grad_high = call(
        third_kernel,
        [((8, LANES), F32), ((9, 8, LANES), F32), ((9, 8, LANES), F32), ((9, 8, LANES), F32)],
        [
            count, facts, slope, onehot, before_one, gate_one, source, slanted, sums, grad_own, back, picked,
            pairs, energy_one, energy_two, radial_in, radial_out_one, mix_one, read_t,
        ],
        scratch=[((4 * C, PAIRS), BF16)],
        limit=24 << 20,
    )
    back = gather_halo(grad_low, grad_mid, grad_high)
    (out,) = call(last_kernel, [((8, LANES), F32)], [grad_mine, back[0], picked])
    out = lax.ppermute(out, AXES, MOVE_OUT)
    forces, energies = call(finish_kernel, [((3, SLOTS), F32), ((1, SLOTS), F32)], [out])
    return forces, energies.reshape(SLOTS)


def solution(mesh):
    whole = P()
    split = P(AXES)
    in_specs = (P(None, AXES), split, split, P(None, AXES), split) + (whole,) * 7
    out_specs = (P(None, AXES), split)
    return jax.shard_map(body, mesh=mesh, in_specs=in_specs, out_specs=out_specs, check_vma=False)
```

```python
import math

import jax
import jax.numpy as jnp
from jax import lax
from jax.experimental import pallas as pl
from jax.experimental.pallas import tpu as pltpu
from jax.sharding import PartitionSpec as P

C = 128
NB = 8
RH = 64
NSPEC = 7
SLOTS = 64
DEPTH = 32
EXPORT = 16
PAIRS = SLOTS * DEPTH
SLAB = 9 * EXPORT
TABLE = 512
LANES = 128
COLUMNS = PAIRS // LANES
DOMAIN_LENGTH = 6.0
CUTOFF = 6.0
SOFTEN = 0.25
NORM = 1.0 / math.sqrt(DEPTH)
AXES = ("gx", "gy", "gz")
F32 = jnp.float32
BF16 = jnp.bfloat16


def dot_nn(a, b):
    return lax.dot_general(a, b, (((1,), (0,)), ((), ())), preferred_element_type=F32)


def dot_nt(a, b):
    return lax.dot_general(a, b, (((1,), (1,)), ((), ())), preferred_element_type=F32)


def dot_tn(a, b):
    return lax.dot_general(a, b, (((0,), (0,)), ((), ())), preferred_element_type=F32)


def iota(shape, dim):
    return lax.broadcasted_iota(jnp.int32, shape, dim)


def column(values, m):
    return values[:, m * LANES : (m + 1) * LANES]


def halves(values):
    high = values.astype(BF16)
    low = (values - high.astype(F32)).astype(BF16)
    return jnp.where(iota(values.shape, 1) % LANES < SLOTS, high.astype(F32), low.astype(F32)).astype(BF16)


def fold(values):
    return values + pltpu.roll(values, SLOTS, 1)


def live_row(count):
    return (iota((1, LANES), 1) % SLOTS < count).astype(F32)


def gather_entries(table, index):
    parts = []
    for m in range(COLUMNS):
        ids = jnp.broadcast_to(column(index, m), (8, LANES))
        low = ids & (LANES - 1)
        high = ids >> 7
        found = jnp.take_along_axis(column(table, 0), low, axis=1)
        for v in range(1, TABLE // LANES):
            found = jnp.where(high == v, jnp.take_along_axis(column(table, v), low, axis=1), found)
        parts.append(found)
    return jnp.concatenate(parts, axis=1)


def sincos_pi(turns):
    whole = jnp.floor(turns + 0.5)
    part = turns - whole
    sign = 1.0 - 2.0 * (whole - 2.0 * jnp.floor(whole * 0.5))
    square = part * part
    sine = 0.0
    cosine = 0.0
    for n in range(6, -1, -1):
        cosine = cosine * square + (-1.0) ** n * math.pi ** (2 * n) / math.factorial(2 * n)
    for n in range(5, -1, -1):
        sine = sine * square + (-1.0) ** n * math.pi ** (2 * n + 1) / math.factorial(2 * n + 1)
    return sine * part * sign, cosine * sign


def geometry(table, index, count):
    found = gather_entries(table, index)
    first = column(table, 0)
    centre = jnp.where(iota((8, LANES), 1) < SLOTS, first, pltpu.roll(first, SLOTS, 1))
    centre = jnp.concatenate([centre] * COLUMNS, axis=1)
    rows = iota((8, PAIRS), 0)
    delta = jnp.where(rows < 3, found - centre, 0.0)
    square = jnp.sum(delta * delta, axis=0, keepdims=True) + SOFTEN
    inverse = lax.rsqrt(square)
    distance = square * inverse
    slot = iota((1, PAIRS), 1) % SLOTS
    paired = jnp.where(index != slot, jnp.concatenate([live_row(count)] * COLUMNS, axis=1), 0.0)
    scaled = jnp.minimum(distance * (1.0 / CUTOFF), 1.0)
    power = scaled * scaled * scaled
    power = power * power
    envelope = 1.0 + power * (-28.0 + scaled * (48.0 - 21.0 * scaled))
    orders = (iota((8, 1), 0) + 1).astype(F32)
    sine, cosine = sincos_pi(orders * scaled)
    weight = envelope * paired * inverse
    basis = (sine * weight).astype(BF16)
    rest = 1.0 - scaled
    slope = (-168.0 / CUTOFF) * (power * rest * rest) / jnp.maximum(scaled, 1e-3)
    basis_slope = weight * cosine * (orders * (math.pi / CUTOFF)) + sine * (
        slope * paired * inverse - weight * inverse
    )
    facts = jnp.where(rows == 3, inverse, jnp.where(rows == 4, found[3:4, :], delta * inverse))
    return facts, basis, basis_slope


def unit_of(facts):
    return jnp.where(iota((8, PAIRS), 0) < 3, facts, 0.0)


def species_of(facts):
    return (iota((16, PAIRS), 0) % 8 == facts[4:5, :].astype(jnp.int32)).astype(F32).astype(BF16)


def split(values):
    high = values.astype(BF16)
    return high, (values - high.astype(F32)).astype(BF16)


def keep(values):
    return values.astype(BF16).astype(F32)


def grad_distance_of(wout, win, grad_radial, before, gate, basis_slope):
    half = grad_radial.shape[0] // 2
    grad_hidden = keep(dot_nn(wout[...], grad_radial[0:half, :]) + dot_nn(wout[...], grad_radial[half:, :]))
    high, low = split(grad_hidden * (gate * (1.0 + before * (1.0 - gate))))
    grad_basis = keep(dot_nn(win, high) + dot_nn(win, low))
    return jnp.sum(grad_basis * basis_slope, axis=0, keepdims=True)


def hidden_of(weights, basis):
    before = dot_nn(weights, basis)
    gate = 1.0 / (1.0 + jnp.exp(-before))
    return before, gate


def pair_gradient(unit, inverse, grad_unit, grad_distance):
    along = jnp.sum(grad_unit * unit, axis=0, keepdims=True)
    return inverse * (grad_unit - unit * along) + unit * grad_distance


def stack_rows(rows):
    where = iota((8, rows[0].shape[1]), 0)
    out = jnp.zeros((8, rows[0].shape[1]), F32)
    for r, row in enumerate(rows):
        out = jnp.where(where == r, row, out)
    return out


def flip(matrix):
    size = matrix.shape[1]
    eye = (iota((size, size), 0) == iota((size, size), 1)).astype(F32).astype(BF16)
    return dot_nt(eye, matrix).astype(BF16)


def fetch(pairs, semaphores):
    copies = [pltpu.make_async_copy(there, here, semaphores.at[k]) for k, (there, here) in enumerate(pairs)]
    for copy in copies:
        copy.start()
    for copy in copies:
        copy.wait()


def weights_kernel(
    embedding_far, radial_in_far, radial_out_one_far, radial_out_two_far, mix_one_far, mix_two_far, readout_far,
    radial_in, radial_out_one, radial_out_two, mix_one, readout,
    emb_t, win_t, one_t, two_t, mix_a, mix_b, mix_two_t, spread, read_t, rests,
    embedding, mix_two, semaphores,
):
    fetch(
        (
            (mix_one_far, mix_one),
            (mix_two_far, mix_two),
            (radial_out_two_far, radial_out_two),
            (radial_out_one_far, radial_out_one),
            (radial_in_far, radial_in),
            (embedding_far, embedding),
            (readout_far, readout),
        ),
        semaphores,
    )
    emb = jnp.concatenate([embedding[...].astype(F32), jnp.zeros((1, C), F32)], axis=0).astype(BF16)
    emb_t[...] = flip(emb)
    for t in range(2):
        win_t[t] = flip(radial_in[t])
        mix_two_t[t] = flip(mix_two[t])
    one_t[...] = flip(radial_out_one[...])
    two_t[...] = flip(radial_out_two[...])
    for k in range(3):
        mix_a[:, k * C : (k + 1) * C] = flip(mix_one[k + 1])
    for k in range(2):
        mix_b[:, k * C : (k + 1) * C] = flip(mix_one[k + 4])
    pe_high, pe_low = split(dot_nt(flip(mix_one[0]), emb))
    spread[...] = jnp.concatenate([pe_high.astype(F32), pe_low.astype(F32)], axis=1).astype(BF16)
    read = jnp.concatenate([readout[...], jnp.zeros((LANES - 2, C), F32)], axis=0)
    read_t[...] = read.T
    read_high, read_low = split(read[0:16])
    for k in range(3):
        rests[k * C : (k + 1) * C, :] = dot_nt(mix_two[k + 2], read_high) + dot_nt(mix_two[k + 2], read_low)


def renamed(index):
    block = (index - SLOTS) >> 4
    nines = (block * 57) >> 9
    threes = (block * 11) >> 5
    turned = (block - threes * 3) * 9 + (threes - nines * 3) * 3 + nines
    return jnp.where(index < SLOTS, index, SLOTS + turned * EXPORT + (index & (EXPORT - 1))).astype(F32)


def pack_kernel(
    counts, exports_far, positions_far, species_far, neighbours_far, packed,
    exports, positions, species, neighbours, semaphores,
):
    fetch(
        (
            (neighbours_far, neighbours),
            (positions_far, positions),
            (species_far, species),
            (exports_far, exports),
        ),
        semaphores,
    )
    even = renamed(neighbours[pl.ds(0, COLUMNS, stride=2), :])
    odd = renamed(neighbours[pl.ds(1, COLUMNS, stride=2), :])
    lane = iota((1, LANES), 1) % EXPORT
    source = jnp.zeros((1, LANES), jnp.int32)
    for e in range(EXPORT):
        source = jnp.where(lane == e, exports[e], source)
    packed[...] = jnp.zeros_like(packed)
    packed[0:COLUMNS, :] = jnp.concatenate([even, odd], axis=1)
    packed[COLUMNS : COLUMNS + 3, 0:SLOTS] = positions[...]
    packed[COLUMNS + 3 : COLUMNS + 4, 0:SLOTS] = species[...].astype(F32)
    packed[COLUMNS + 4 : COLUMNS + 5, :] = source.astype(F32)
    packed[COLUMNS + 5 : COLUMNS + 6, :] = jnp.full((1, LANES), counts[0], jnp.int32).astype(F32)


def unpack_kernel(arrived, own, payload, picked, index, count):
    whole = arrived[COLUMNS : COLUMNS + 8, :]
    whole = jnp.where(iota((8, LANES), 0) < 4, whole, 0.0)
    own[...] = whole
    exports = arrived[COLUMNS + 4 : COLUMNS + 5, :]
    count[...] = arrived[COLUMNS + 5 : COLUMNS + 6, :].astype(jnp.int32)
    mine = iota((EXPORT, LANES), 1) == iota((EXPORT, LANES), 0)
    pick = jnp.sum(jnp.where(mine, exports, 0.0), axis=1, keepdims=True)
    picked[...] = jnp.broadcast_to(pick, (EXPORT, LANES)).astype(jnp.int32)
    source = jnp.broadcast_to(exports, (8, LANES)).astype(jnp.int32)
    payload[0] = jnp.take_along_axis(whole, source, axis=1)
    for m in range(COLUMNS):
        index[:, m * LANES : (m + 1) * LANES] = arrived[m : m + 1, :].astype(jnp.int32)


def side_kernel(
    facts_ref, basis, index, win_t, one_t, spread,
    onehot, before_one, gate_one, before_two, gate_two, source, slanted,
):
    ids = index[...]
    entry = iota((TABLE, LANES), 0)
    for m in range(COLUMNS):
        onehot[:, m * LANES : (m + 1) * LANES] = (entry == column(ids, m)).astype(F32).astype(BF16)
    before, gate = hidden_of(win_t[1], basis[...])
    before_two[...] = before
    gate_two[...] = gate
    before, gate = hidden_of(win_t[0], basis[...])
    before_one[...] = before
    gate_one[...] = gate
    hidden = (before * gate).astype(BF16)
    species = species_of(facts_ref[...])
    for m in range(COLUMNS):
        here = slice(m * LANES, (m + 1) * LANES)
        found = dot_nn(spread[...], column(species, m))
        source[:, here] = found
        slanted[:, here] = found * dot_nn(one_t[C : 2 * C, :], column(hidden, m))


def first_kernel(
    count_ref, own, low, mid, high, index, picked, win_t, wout_t, mix_a, mix_b, spread, emb_t, read_t,
    facts_out, basis_out, slope_out, own_rows, outgoing, sums, energy,
):
    count = count_ref[...]
    group = iota((8, LANES), 1) // EXPORT
    rows8 = iota((8, 1), 0)
    tiles = [own[...]] + [jnp.zeros((8, LANES), F32) for _ in range(3)]
    slabs = (low, mid, high)
    for b in range(27):
        oz, oy, ox = b // 9 - 1, b // 3 % 3 - 1, b % 3 - 1
        entry = SLOTS + b * EXPORT
        shift = jnp.where(rows8 == 0, DOMAIN_LENGTH * ox, 0.0)
        shift = jnp.where(rows8 == 1, DOMAIN_LENGTH * oy, shift)
        shift = jnp.where(rows8 == 2, DOMAIN_LENGTH * oz, shift)
        tile = entry // LANES
        at = entry % LANES // EXPORT
        tiles[tile] = jnp.where(group == at, slabs[oz + 1][b % 9] + shift, tiles[tile])
    whole = jnp.concatenate(tiles, axis=1)
    facts, basis, basis_slope = geometry(whole, index[...], count)
    facts_out[...] = facts
    basis_out[...] = basis
    slope_out[...] = basis_slope
    before, gate = hidden_of(win_t[0], basis)
    hidden = (before * gate).astype(BF16)
    species = species_of(facts)
    a0 = jnp.zeros((C, LANES), F32)
    a1 = [jnp.zeros((C, LANES), F32) for _ in range(3)]
    for m in range(COLUMNS):
        radial = dot_nn(wout_t[...], column(hidden, m))
        source = dot_nn(spread[...], column(species, m))
        a0 = a0 + radial[:C] * source
        t = radial[C:] * source
        for x in range(3):
            a1[x] = a1[x] + t * column(facts[x : x + 1], m)
    a0 = fold(a0) * NORM
    a1 = [fold(v) * NORM for v in a1]
    for x, v in enumerate([a0] + a1):
        sums[x * C : (x + 1) * C, :] = v
    quad = a1[0] * a1[0] + a1[1] * a1[1] + a1[2] * a1[2]
    own_kind = (iota((8, LANES), 0) == whole[3:4, :LANES].astype(jnp.int32)).astype(F32).astype(BF16)
    own_kind = jnp.where(iota((8, LANES), 1) < SLOTS, own_kind.astype(F32), 0.0).astype(BF16)
    scalar = dot_nn(emb_t[...], own_kind)
    scalar = scalar + dot_nn(mix_a[...], jnp.concatenate([halves(a0), halves(a0 * a0), halves(quad)], axis=0))
    scalar = fold(scalar)
    top = jnp.concatenate([halves(v) for v in a1], axis=1)
    bottom = jnp.concatenate([halves(a0 * v) for v in a1], axis=1)
    vector = dot_nn(mix_b[...], jnp.concatenate([top, bottom], axis=0))
    parts = [scalar] + [fold(column(vector, x)) for x in range(3)]
    features = jnp.concatenate(parts, axis=0).astype(BF16)
    rounded = features[:C].astype(F32)
    row_energy = jnp.sum(scalar * read_t[:, 0:1] + rounded * read_t[:, 1:2], axis=0, keepdims=True)
    energy[...] = row_energy * live_row(count)
    lanes = iota((SLOTS, LANES), 1)
    eye = (lanes == iota((SLOTS, LANES), 0)).astype(F32).astype(BF16)
    chosen = (iota((EXPORT, LANES), 1) == picked[...]).astype(F32).astype(BF16)
    own_rows[...] = dot_nt(eye, features).astype(BF16)
    outgoing[...] = dot_nt(chosen, features).astype(BF16)


def second_kernel(
    count_ref, facts_ref, onehot, before_two, gate_two, own_rows, low, mid, high, wout_t, mix_t, rests, read,
    grad_own, grad_low, grad_mid, grad_high, grad_radial, grad_unit, energy,
    feats, turned, radial, source, grad_source,
):
    count = count_ref[...]
    facts = facts_ref[...]
    hidden = (before_two[...] * gate_two[...]).astype(BF16)
    feats[0:SLOTS, :] = own_rows[...]
    feats[SLOTS : SLOTS + SLAB, :] = low[...]
    feats[SLOTS + SLAB : SLOTS + 2 * SLAB, :] = mid[...]
    feats[SLOTS + 2 * SLAB : SLOTS + 3 * SLAB, :] = high[...]
    feats[SLOTS + 3 * SLAB :, :] = jnp.zeros((TABLE - SLOTS - 3 * SLAB, 4 * C), BF16)
    eye = (iota((C, C), 0) == iota((C, C), 1)).astype(F32).astype(BF16)
    for c in range(4):
        turned[c * C : (c + 1) * C, :] = dot_nt(eye, feats[:, c * C : (c + 1) * C]).astype(BF16)
    units = [[column(facts[x : x + 1], m) for m in range(COLUMNS)] for x in range(3)]
    wide = 2 * LANES
    a0 = jnp.zeros((C, LANES), F32)
    a1 = [jnp.zeros((C, LANES), F32) for _ in range(3)]
    for w in range(PAIRS // wide):
        at = slice(w * wide, (w + 1) * wide)
        radial[:, at] = dot_nn(wout_t[...], hidden[:, at])
        picked = dot_nn(turned[...], onehot[:, at]).astype(BF16)
        for c in range(4):
            source[c * C : (c + 1) * C, at] = dot_nn(mix_t[min(c, 1)], picked[c * C : (c + 1) * C])
        for m in (2 * w, 2 * w + 1):
            here = slice(m * LANES, (m + 1) * LANES)
            s = source[0:C, here]
            v = [source[(x + 1) * C : (x + 2) * C, here] for x in range(3)]
            u = [units[x][m] for x in range(3)]
            along = v[0] * u[0] + v[1] * u[1] + v[2] * u[2]
            a0 = a0 + radial[0:C, here] * s + radial[3 * C :, here] * along
            t = radial[C : 2 * C, here] * s
            r3 = radial[2 * C : 3 * C, here]
            for x in range(3):
                a1[x] = a1[x] + t * u[x] + r3 * v[x]
    a0 = fold(a0) * NORM
    a1 = [fold(v) * NORM for v in a1]
    quad = a1[0] * a1[0] + a1[1] * a1[1] + a1[2] * a1[2]
    m2, m3, m4 = [rests[k * C : (k + 1) * C, 1:2] for k in range(3)]
    live = live_row(count)
    energy[...] = live * jnp.sum(a0 * m2 + a0 * a0 * m3 + quad * m4, axis=0, keepdims=True)
    live = live * NORM
    d0 = (m2 + 2.0 * a0 * m3) * live
    d1 = [2.0 * v * m4 * live for v in a1]
    grad_units = [[], [], []]
    for m in range(COLUMNS):
        here = slice(m * LANES, (m + 1) * LANES)
        s = source[0:C, here]
        v = [source[(x + 1) * C : (x + 2) * C, here] for x in range(3)]
        u = [units[x][m] for x in range(3)]
        r1, r2, r3, r4 = [radial[k * C : (k + 1) * C, here] for k in range(4)]
        along = v[0] * u[0] + v[1] * u[1] + v[2] * u[2]
        slant = d1[0] * u[0] + d1[1] * u[1] + d1[2] * u[2]
        parts = (d0 * s, s * slant, d1[0] * v[0] + d1[1] * v[1] + d1[2] * v[2], d0 * along)
        for k in range(4):
            high_part, low_part = split(parts[k])
            grad_radial[k * C : (k + 1) * C, here] = high_part
            grad_radial[(k + 4) * C : (k + 5) * C, here] = low_part
        grad_source[0:C, here] = (r1 * d0 + r2 * slant).astype(BF16)
        q = d0 * r4
        t = r2 * s
        for x in range(3):
            grad_source[(x + 1) * C : (x + 2) * C, here] = (q * u[x] + r3 * d1[x]).astype(BF16)
            grad_units[x].append(jnp.sum(q * v[x] + t * d1[x], axis=0, keepdims=True))
    grad_unit[...] = stack_rows([jnp.concatenate(g, axis=1) for g in grad_units])
    grad_projected = dot_nt(onehot[...], grad_source[...])
    outs = (grad_low, grad_mid, grad_high)
    live_rows = (iota((SLOTS, 1), 0) < count[:, 0:1]).astype(F32)
    for c in range(4):
        at = slice(c * C, (c + 1) * C)
        high_part, low_part = split(grad_projected[:, at])
        rows = dot_nn(high_part, mix_t[min(c, 1)]) + dot_nn(low_part, mix_t[min(c, 1)])
        mine = rows[0:SLOTS]
        if c == 0:
            mine = mine + live_rows * read[1:2, :]
        grad_own[:, at] = mine
        for k in range(3):
            begin = SLOTS + k * SLAB
            outs[k][:, at] = rows[begin : begin + SLAB].astype(BF16)


def pairs_kernel(facts_ref, slope, before, gate, grad_radial, grad_unit, wout, win, pair_out):
    facts = facts_ref[...]
    grad_distance = grad_distance_of(wout, win[1], grad_radial, before[...], gate[...], slope[...])
    pair_out[...] = pair_gradient(unit_of(facts), facts[3:4, :], grad_unit[...], grad_distance)


def third_kernel(
    count_ref, facts_ref, slope, onehot, before_one, gate_one, sources, slanted, sums, grad_own, back, picked,
    pair_in, energy_one, energy_two, win, wout, mix_one, read_t,
    grad_mine, grad_low, grad_mid, grad_high,
    grad_radial,
):
    count = count_ref[...]
    facts = facts_ref[...]
    unit, inverse = unit_of(facts), facts[3:4, :]
    before, gate = before_one[...], gate_one[...]
    mine = grad_own[...]
    mine_high = mine.astype(BF16)
    mine_low = (mine - mine_high.astype(F32)).astype(BF16)
    came = back[...].astype(F32)
    came_high = came.astype(BF16)
    came_low = (came - came_high.astype(F32)).astype(BF16)
    eye = (iota((SLOTS, LANES), 1) % SLOTS == iota((SLOTS, LANES), 0)).astype(F32).astype(BF16)
    chosen = (iota((EXPORT, LANES), 1) % SLOTS == picked[...]).astype(F32).astype(BF16)
    left = jnp.concatenate([mine_high, mine_low, came_high, came_low], axis=0)
    right = jnp.concatenate([eye, eye, chosen, chosen], axis=0)
    grads = dot_tn(left, right)
    live = live_row(count)
    gs = grads[0:C] + read_t[:, 0:1] * live
    gv = [grads[(x + 1) * C : (x + 2) * C] for x in range(3)]
    a0 = sums[0:C, :]
    a1 = [sums[(x + 1) * C : (x + 2) * C, :] for x in range(3)]
    scalar_parts = halves(gs)
    vector_parts = jnp.concatenate([halves(g) for g in gv], axis=1)
    first = jnp.concatenate([fold(dot_nn(mix_one[k], scalar_parts)) for k in (1, 2, 3)], axis=0)
    others = jnp.concatenate([fold_columns(dot_nn(mix_one[k], vector_parts)) for k in (4, 5)], axis=0)
    straight = [column(others[0:C], x) for x in range(3)]
    crossed = [column(others[C : 2 * C], x) for x in range(3)]
    scale = live * NORM
    d0 = first[0:C] + 2.0 * a0 * first[C : 2 * C]
    for x in range(3):
        d0 = d0 + a1[x] * crossed[x]
    d0 = d0 * scale
    d1 = [(straight[x] + a0 * crossed[x] + 2.0 * a1[x] * first[2 * C : 3 * C]) * scale for x in range(3)]
    grad_units = [[], [], []]
    for m in range(COLUMNS):
        here = slice(m * LANES, (m + 1) * LANES)
        source = sources[:, here]
        u = [column(unit[x : x + 1], m) for x in range(3)]
        slant = d1[0] * u[0] + d1[1] * u[1] + d1[2] * u[2]
        parts = (d0 * source, slant * source)
        for k in range(2):
            high_part, low_part = split(parts[k])
            grad_radial[k * C : (k + 1) * C, here] = high_part
            grad_radial[(k + 2) * C : (k + 3) * C, here] = low_part
        q = slanted[:, here]
        for x in range(3):
            grad_units[x].append(jnp.sum(q * d1[x], axis=0, keepdims=True))
    grad_unit = stack_rows([jnp.concatenate(g, axis=1) for g in grad_units])
    grad_distance = grad_distance_of(wout, win[0], grad_radial, before, gate, slope[...])
    pairs = pair_in[...] + pair_gradient(unit, inverse, grad_unit, grad_distance)
    pair_high = pairs.astype(BF16)
    pair_low = (pairs - pair_high.astype(F32)).astype(BF16)
    both = jnp.concatenate([pair_high.astype(F32), pair_low.astype(F32)], axis=0).astype(BF16)
    spread_back = dot_nt(both, onehot[...])
    grads = spread_back[0:8] + spread_back[8:16]
    total = column(pairs, 0)
    for m in range(1, COLUMNS):
        total = total + column(pairs, m)
    energies = live * (energy_one[...] + energy_two[...])
    grad_mine[...] = jnp.where(iota((8, LANES), 0) == 3, energies, column(grads, 0) - fold(total))
    outs = (grad_low, grad_mid, grad_high)
    for b in range(27):
        at = SLOTS + b * EXPORT
        tile = column(grads, at // LANES)
        offset = at % LANES
        if offset:
            tile = pltpu.roll(tile, LANES - offset, 1)
        outs[b // 9][b % 9] = tile


def fold_columns(values):
    count = values.shape[1] // LANES
    return jnp.concatenate([fold(column(values, x)) for x in range(count)], axis=1)


def last_kernel(grad_mine, back, picked, out):
    same = iota((EXPORT, LANES), 1) == picked[...]
    entry = jnp.sum(jnp.where(same, iota((EXPORT, LANES), 0), 0), axis=0, keepdims=True)
    hit = jnp.sum(same.astype(F32), axis=0, keepdims=True)
    came = jnp.take_along_axis(back[...], jnp.broadcast_to(entry, (8, LANES)), axis=1)
    mine = grad_mine[...]
    out[...] = jnp.where(iota((8, LANES), 0) == 3, mine, -(mine + came * hit))


def finish_kernel(out, forces, energies):
    forces[...] = out[0:3, 0:SLOTS]
    energies[...] = out[3:4, 0:SLOTS]


def call(kernel, outs, specs, scratch=(), limit=None, far=False, cost=None):
    spaces = [pltpu.HBM if far else pltpu.VMEM] * len(specs)
    if far:
        spaces = [space if v.size > 1 else pltpu.SMEM for space, v in zip(spaces, specs)]
        specs = [pltpu.with_memory_space_constraint(v, pltpu.HBM) if v.size > 1 else v for v in specs]
    return pl.pallas_call(
        kernel,
        out_shape=[jax.ShapeDtypeStruct(s, t) for s, t in outs],
        in_specs=[pl.BlockSpec(memory_space=space) for space in spaces],
        out_specs=[pl.BlockSpec(memory_space=pltpu.VMEM)] * len(outs),
        scratch_shapes=[s if not isinstance(s, tuple) else pltpu.VMEM(*s) for s in scratch],
        compiler_params=pltpu.CompilerParams(vmem_limit_bytes=limit or (16 << 20)),
        cost_estimate=cost,
    )(*specs)


DOMAINS = [(x, y, z) for x in range(16) for y in range(4) for z in range(8)]


def given(x, y, z):
    return (x * 4 + y) * 8 + z


def seat(x, y, z):
    x, y, z = (1 - x) % 16, y % 4, (z + 5) % 8
    return given(z // 2 * 4 + x // 8 * 2 + z % 2, y, x % 8)


MOVE_IN = [(given(*d), seat(*d)) for d in DOMAINS]
MOVE_OUT = [(there, here) for here, there in MOVE_IN]


def moves(step):
    return [(seat(*d), seat(*(a + b for a, b in zip(d, step)))) for d in DOMAINS]


UP = ((1, 0, 0), (0, 1, 0), (0, 0, 1))
DOWN = ((-1, 0, 0), (0, -1, 0), (0, 0, -1))


def send(value, step):
    return lax.ppermute(value, AXES, moves(step))


def spread_halo(block):
    for axis in range(2):
        low = send(block, UP[axis])
        high = send(block, DOWN[axis])
        block = jnp.concatenate([low, block, high], axis=0)
    return send(block, UP[2]), block, send(block, DOWN[2])


def gather_halo(low, mid, high):
    for axis in (2, 1, 0):
        from_low = send(high, UP[axis])
        from_high = send(low, DOWN[axis])
        block = mid + from_low + from_high
        if axis:
            third = block.shape[0] // 3
            low, mid, high = block[:third], block[third : 2 * third], block[2 * third :]
    return block


def body(
    positions, species, counts, neighbours, exports, embedding, radial_in,
    radial_out_one, radial_out_two, mix_one, mix_two, readout,
):
    (packed,) = call(
        pack_kernel,
        [((24, LANES), F32)],
        [counts, exports, positions, species.reshape(1, SLOTS), neighbours],
        scratch=[
            pltpu.SMEM((EXPORT,), jnp.int32),
            ((3, SLOTS), F32),
            ((1, SLOTS), jnp.int32),
            ((DEPTH, SLOTS), jnp.int32),
            pltpu.SemaphoreType.DMA((4,)),
        ],
        far=True,
    )
    weights = call(
        weights_kernel,
        [
            ((2, NB, RH), BF16),
            ((RH, 2 * C), BF16),
            ((RH, 4 * C), BF16),
            ((6, C, C), BF16),
            ((2, C), F32),
            ((C, 8), BF16),
            ((2, RH, NB), BF16),
            ((2 * C, RH), BF16),
            ((4 * C, RH), BF16),
            ((C, 3 * C), BF16),
            ((C, 2 * C), BF16),
            ((2, C, C), BF16),
            ((C, 16), BF16),
            ((C, LANES), F32),
            ((3 * C, 16), F32),
        ],
        [embedding, radial_in, radial_out_one, radial_out_two, mix_one, mix_two, readout],
        scratch=[((NSPEC, C), BF16), ((5, C, C), BF16), pltpu.SemaphoreType.DMA((7,))],
        far=True,
        cost=pl.CostEstimate(flops=200_000_000, bytes_accessed=2_000_000, transcendentals=0),
    )
    arrived = lax.ppermute(packed, AXES, MOVE_IN)
    (
        radial_in, radial_out_one, radial_out_two, mix_one, readout,
        emb_t, win_t, one_t, two_t, mix_a, mix_b, mix_two_t, spread, read_t, rests,
    ) = weights
    own, payload, picked, index, count = call(
        unpack_kernel,
        [
            ((8, LANES), F32),
            ((1, 8, LANES), F32),
            ((EXPORT, LANES), jnp.int32),
            ((1, PAIRS), jnp.int32),
            ((1, LANES), jnp.int32),
        ],
        [arrived],
    )
    low, mid, high = spread_halo(payload)
    facts, basis, slope, own_rows, outgoing, sums, energy_one = call(
        first_kernel,
        [
            ((8, PAIRS), F32),
            ((8, PAIRS), BF16),
            ((8, PAIRS), F32),
            ((SLOTS, 4 * C), BF16),
            ((EXPORT, 4 * C), BF16),
            ((4 * C, LANES), F32),
            ((1, LANES), F32),
        ],
        [count, own, low, mid, high, index, picked, win_t, one_t, mix_a, mix_b, spread, emb_t, read_t],
    )
    onehot, before_one, gate_one, before_two, gate_two, source, slanted = call(
        side_kernel,
        [
            ((TABLE, PAIRS), BF16),
            ((RH, PAIRS), F32),
            ((RH, PAIRS), F32),
            ((RH, PAIRS), F32),
            ((RH, PAIRS), F32),
            ((C, PAIRS), F32),
            ((C, PAIRS), F32),
        ],
        [facts, basis, index, win_t, one_t, spread],
        cost=pl.CostEstimate(flops=500_000_000, bytes_accessed=6_000_000, transcendentals=0),
    )
    low, mid, high = spread_halo(outgoing)
    grad_own, grad_low, grad_mid, grad_high, grad_radial, grad_unit, energy_two = call(
        second_kernel,
        [
            ((SLOTS, 4 * C), F32),
            ((SLAB, 4 * C), BF16),
            ((SLAB, 4 * C), BF16),
            ((SLAB, 4 * C), BF16),
            ((8 * C, PAIRS), BF16),
            ((8, PAIRS), F32),
            ((1, LANES), F32),
        ],
        [
            count, facts, onehot, before_two, gate_two, own_rows, low, mid, high, two_t, mix_two_t, rests, readout,
        ],
        scratch=[
            ((TABLE, 4 * C), BF16),
            ((4 * C, TABLE), BF16),
            ((4 * C, PAIRS), F32),
            ((4 * C, PAIRS), F32),
            ((4 * C, PAIRS), BF16),
        ],
        limit=30 << 20,
    )
    (pairs,) = call(
        pairs_kernel,
        [((8, PAIRS), F32)],
        [facts, slope, before_two, gate_two, grad_radial, grad_unit, radial_out_two, radial_in],
        cost=pl.CostEstimate(flops=500_000_000, bytes_accessed=6_000_000, transcendentals=0),
    )
    back = gather_halo(grad_low, grad_mid, grad_high)
    grad_mine, grad_low, grad_mid, grad_high = call(
        third_kernel,
        [((8, LANES), F32), ((9, 8, LANES), F32), ((9, 8, LANES), F32), ((9, 8, LANES), F32)],
        [
            count, facts, slope, onehot, before_one, gate_one, source, slanted, sums, grad_own, back, picked,
            pairs, energy_one, energy_two, radial_in, radial_out_one, mix_one, read_t,
        ],
        scratch=[((4 * C, PAIRS), BF16)],
        limit=24 << 20,
    )
    back = gather_halo(grad_low, grad_mid, grad_high)
    (out,) = call(last_kernel, [((8, LANES), F32)], [grad_mine, back[0], picked])
    out = lax.ppermute(out, AXES, MOVE_OUT)
    forces, energies = call(finish_kernel, [((3, SLOTS), F32), ((1, SLOTS), F32)], [out])
    return forces, energies.reshape(SLOTS)


def solution(mesh):
    whole = P()
    split = P(AXES)
    in_specs = (P(None, AXES), split, split, P(None, AXES), split) + (whole,) * 7
    out_specs = (P(None, AXES), split)
    return jax.shard_map(body, mesh=mesh, in_specs=in_specs, out_specs=out_specs, check_vma=False)
```
